256 devices in a mesh: dom: 128 (over z, y, x), ord: 2 (over core).
Axes of the slice: x: 4, y: 4, z: 8, core: 2. Of those that a mesh axis runs over, the one named last changes fastest.
Arguments:
- polar_images: bfloat16 [1024, 128, 512], P(('dom', 'ord')), may hold values from -6 to 6
- radial_basis: bfloat16 [256, 128, 128], P('ord'), may hold values from -0.5 to 0.5
- radial_start: int32 [256], P('ord'), may hold values from 0 to 4, as said below
- radial_count: int32 [256], P('ord'), may hold values from 32 to 128
- order_of_slot: int32 [256], replicated, may hold values from 0 to 255, each once
- start_block: float32 [256, 16, 128], P('ord'), may hold values from -6 to 6
Outputs:
- denoised: bfloat16 [1024, 128, 512], P(('dom', 'ord'))
The draws below stay inside these ranges and needn't reach their ends.
Inputs may be any that keep to these rules, and one draw needn't show every extreme that they name: `radial_start`: every slot keeps at least 64 radial samples.
All inputs are finite; a program needn't handle non-finite values.
Results may differ from the reference program's by a relative error of at most 0.01.
Values may be sent and summed in bfloat16 or wider, within the bound.
A program may use at most 64 MiB of HBM per device.

```python
import math
import jax
import jax.numpy as jnp
from jax import lax

NR = 128
NT = 512
K = 256
QMAX = 128
R = 16
NRB = 8
ITERS = 4
PARTICLES = 1024


def draw_radial_count(key, part):
    counts = jax.random.randint(jax.random.fold_in(key, 11), (K,), 2 * R, QMAX + 1)
    picked = jax.random.randint(jax.random.fold_in(key, 12), (), 0, K)
    return jnp.where(jnp.arange(K) == picked, QMAX, counts).astype(jnp.int32)


def draw_radial_start(key, part):
    starts = jax.random.randint(jax.random.fold_in(key, 21), (K,), 0, NRB // 2 + 1)
    picked = jax.random.randint(jax.random.fold_in(key, 22), (), 0, K)
    slot_ids = jnp.arange(K)
    starts = jnp.where(slot_ids == picked, NRB // 2, starts)
    starts = jnp.where(slot_ids == (picked + 1) % K, 0, starts)
    return starts.astype(jnp.int32)


def steps_of(own_key, shape, split, low, high):
    def one(dim, blocks):
        heights = jax.random.uniform(jax.random.fold_in(jax.random.fold_in(own_key, 6), dim), (blocks,), jnp.float32, low / len(split), high / len(split))
        return jnp.repeat(jnp.exp(heights), shape[dim] // blocks).reshape((-1,) + (1,) * (len(shape) - dim - 1))

    factor_of = one(*split[0])
    for cut in split[1:]:
        factor_of = factor_of * one(*cut)
    return factor_of


def normal_values(stream_key, extent, width, limit, shards=(), kind=jnp.bfloat16):
    drawn = width * jax.random.normal(stream_key, extent, jnp.float32)
    if shards:
        drawn = drawn * steps_of(stream_key, extent, shards, -0.22, 0.18)
    return jnp.clip(drawn, -limit, limit).astype(kind)


def setup_inputs(seed: int = 0) -> dict:
    key_list = jax.random.split(jax.random.key(seed), 7)
    polar_images = normal_values(key_list[0], (PARTICLES, NR, NT), 1.0, 6.0, ((0, 256),))
    radial_basis = normal_values(key_list[1], (K, NR, QMAX), NR ** -0.5, 0.5, ((0, 2),))
    radial_start = draw_radial_start(jax.random.fold_in(key_list[6], 71), 0)
    radial_count = draw_radial_count(jax.random.fold_in(key_list[6], 71), 0)
    order_of_slot = jax.random.permutation(key_list[4], K).astype(jnp.int32)
    start_block = normal_values(key_list[5], (K, R, QMAX), 1.0, 6.0, ((0, 2),), jnp.float32)
    return dict(polar_images=polar_images, radial_basis=radial_basis, radial_start=radial_start, radial_count=radial_count, order_of_slot=order_of_slot, start_block=start_block)


def make_table(order_of_slot, angles):
    steps_t = jnp.arange(angles, dtype=jnp.int32)
    phase_int = steps_t[:, None] * order_of_slot[None, :].astype(jnp.int32) % angles
    radians = phase_int.astype(jnp.float32) * (2.0 * math.pi / angles)
    weight = math.sqrt(2.0 / angles)
    paired = jnp.stack([jnp.cos(radians) * weight, -jnp.sin(radians) * weight], axis=2)
    return paired.reshape(angles, -1).astype(jnp.bfloat16)

def masked_basis(radial_basis, radial_start, radial_count, blocks):
    radial_rows = radial_basis.shape[1]
    slot_cols = radial_basis.shape[2]
    row_ids = jnp.arange(radial_rows, dtype=jnp.int32)
    col_ids = jnp.arange(slot_cols, dtype=jnp.int32)
    keep_rows = row_ids[None, :, None] >= radial_start[:, None, None] * (radial_rows // blocks)
    keep_cols = col_ids[None, None, :] < radial_count[:, None, None]
    return jnp.where(keep_rows & keep_cols, radial_basis, jnp.zeros_like(radial_basis))

def subspace(cov_mat, start_t):
    basis_t = start_t
    for step in range(ITERS):
        image_t = jnp.einsum('srm,smq->srq', basis_t, cov_mat, precision=lax.Precision.HIGHEST)
        gram_matrix = jnp.einsum('srq,stq->srt', image_t, image_t, precision=lax.Precision.HIGHEST)
        factor = jnp.linalg.cholesky(gram_matrix)
        basis_t = jax.scipy.linalg.solve_triangular(factor, image_t, lower=True)
    return basis_t

def reference(polar_images, radial_basis, radial_start, radial_count, order_of_slot, start_block):
    dft_table = make_table(order_of_slot, NT)
    spectrum = jnp.dot(polar_images.reshape(PARTICLES * NR, NT).astype(jnp.float32), dft_table.astype(jnp.float32), preferred_element_type=jnp.float32)
    spectrum = spectrum.astype(jnp.bfloat16).reshape(PARTICLES, NR, K, 2)
    masked = masked_basis(radial_basis, radial_start, radial_count, NRB)
    coef_four = jnp.einsum('prsc,srq->scpq', spectrum.astype(jnp.float32), masked.astype(jnp.float32)).astype(jnp.bfloat16)
    coef_rows = coef_four.reshape(K, 2 * PARTICLES, QMAX).astype(jnp.float32)
    cov_all = jnp.einsum('snq,snm->sqm', coef_rows, coef_rows)
    eig_t = subspace(cov_all, start_block.astype(jnp.float32)).astype(jnp.bfloat16)
    u_t = jnp.einsum('stq,srq->str', eig_t.astype(jnp.float32), masked.astype(jnp.float32)).astype(jnp.bfloat16)
    scores = jnp.einsum('scpq,stq->psct', coef_four.astype(jnp.float32), eig_t.astype(jnp.float32)).astype(jnp.bfloat16)
    profile = jnp.einsum('psct,str->prsc', scores.astype(jnp.float32), u_t.astype(jnp.float32)).astype(jnp.bfloat16)
    profile = profile.reshape(PARTICLES * NR, 2 * K)
    denoised = lax.dot_general(profile.astype(jnp.float32), dft_table.astype(jnp.float32), (((1,), (1,)), ((), ())), preferred_element_type=jnp.float32)
    return denoised.astype(jnp.bfloat16).reshape(PARTICLES, NR, NT)
```

```python
import functools
import math

import jax
import jax.numpy as jnp
from jax import lax
from jax.experimental import pallas as pl
from jax.experimental.pallas import tpu as pltpu
from jax.sharding import PartitionSpec as P

NRB = 8
ITERS = 4
NZ, NY, NX = 8, 4, 4
NDOM = NZ * NY * NX
NDEV = 2 * NDOM
MESH = pl.DeviceIdType.MESH


def make_table(order_of_slot, angles):
    steps_t = jnp.arange(angles, dtype=jnp.int32)
    phase_int = order_of_slot[:, None] * steps_t[None, :] % angles
    radians = phase_int.astype(jnp.float32) * (2.0 * math.pi / angles)
    weight = math.sqrt(2.0 / angles)
    return jnp.stack([jnp.cos(radians) * weight, -jnp.sin(radians) * weight]).astype(jnp.bfloat16)


def orthonormal(image_t):
    gram_matrix = jnp.einsum("srq,stq->srt", image_t, image_t, precision=lax.Precision.HIGHEST)
    factor = jnp.linalg.cholesky(gram_matrix)
    return jax.scipy.linalg.solve_triangular(factor, image_t, lower=True)


def subspace(cov_mat, start_t):
    basis_t = start_t
    for step in range(ITERS):
        image_t = jnp.einsum("srm,smq->srq", basis_t, cov_mat, precision=lax.Precision.HIGHEST)
        basis_t = orthonormal(image_t)
    return basis_t


def exchange_kernel(src_ref, dst_ref, send_sem, recv_sem, own_sem):
    d = lax.axis_index("dom")
    o = lax.axis_index("ord")
    z, y, x = d // (NY * NX), (d // NX) % NY, d % NX
    mine = o * NDOM + d

    def peer(i):
        pz = (z + i % NZ) % NZ
        py = (y + (i // NZ) % NY) % NY
        px = (x + (i // (NZ * NY)) % NX) % NX
        po = (o + i // NDOM) % 2
        return (pz * NY + py) * NX + px, po

    barrier = pltpu.get_barrier_semaphore()

    def greet(i, carry):
        pl.semaphore_signal(barrier, inc=1, device_id=peer(i), device_id_type=MESH)
        return carry

    lax.fori_loop(1, NDEV, greet, 0)
    own = pltpu.make_async_copy(src_ref.at[mine], dst_ref.at[mine], own_sem)
    own.start()
    pl.semaphore_wait(barrier, NDEV - 1)

    def send(i, carry):
        pd, po = peer(i)
        pltpu.make_async_remote_copy(
            src_ref=src_ref.at[po * NDOM + pd],
            dst_ref=dst_ref.at[mine],
            send_sem=send_sem,
            recv_sem=recv_sem,
            device_id=(pd, po),
            device_id_type=MESH,
        ).start()
        return carry

    lax.fori_loop(1, NDEV, send, 0)
    own.wait()
    most = pl.ds(0, NDEV - 1)
    everything = pltpu.make_async_remote_copy(
        src_ref=src_ref.at[most],
        dst_ref=dst_ref.at[most],
        send_sem=send_sem,
        recv_sem=recv_sem,
        device_id=(d, 1 - o),
        device_id_type=MESH,
    )
    everything.wait_send()
    everything.wait_recv()


def exchange(blocks, collective_id):
    return pl.pallas_call(
        exchange_kernel,
        out_shape=jax.ShapeDtypeStruct(blocks.shape, blocks.dtype),
        in_specs=[pl.BlockSpec(memory_space=pltpu.VMEM)],
        out_specs=pl.BlockSpec(memory_space=pltpu.VMEM),
        scratch_shapes=[pltpu.SemaphoreType.DMA, pltpu.SemaphoreType.DMA, pltpu.SemaphoreType.DMA],
        compiler_params=pltpu.CompilerParams(collective_id=collective_id, has_side_effects=True),
        name=f"exchange_{collective_id}",
    )(blocks)


def on_device(polar_images, radial_basis, radial_start, radial_count, order_of_slot, start_block):
    particles, radial_rows, angles = polar_images.shape
    table = make_table(order_of_slot, angles)
    spectrum = jnp.einsum(
        "cst,prt->scpr", table, polar_images, preferred_element_type=jnp.float32
    ).astype(jnp.bfloat16)
    rows = exchange(spectrum.reshape(NDEV, 2 * particles, radial_rows), 0)
    rows = rows.reshape(NDEV * 2 * particles, radial_rows)

    slot = lax.axis_index("dom")
    basis = lax.dynamic_index_in_dim(radial_basis, slot, 0, keepdims=False)
    first_row = lax.dynamic_index_in_dim(radial_start, slot, 0, keepdims=False) * (radial_rows // NRB)
    count = lax.dynamic_index_in_dim(radial_count, slot, 0, keepdims=False)
    start_t = lax.dynamic_index_in_dim(start_block, slot, 0, keepdims=True)
    keep_rows = jnp.arange(radial_rows)[:, None] >= first_row
    keep_cols = jnp.arange(basis.shape[1])[None, :] < count
    masked = jnp.where(keep_rows & keep_cols, basis, jnp.zeros_like(basis))

    coef = jnp.dot(rows, masked, preferred_element_type=jnp.float32).astype(jnp.bfloat16)
    cov = jnp.einsum("nq,nm->qm", coef, coef, preferred_element_type=jnp.float32)
    eig_t = subspace(cov[None], start_t)[0].astype(jnp.bfloat16)
    u_t = jnp.einsum("tq,rq->tr", eig_t, masked, preferred_element_type=jnp.float32).astype(jnp.bfloat16)
    scores = jnp.einsum("nq,tq->nt", coef, eig_t, preferred_element_type=jnp.float32).astype(jnp.bfloat16)
    profile = jnp.dot(scores, u_t, preferred_element_type=jnp.float32).astype(jnp.bfloat16)

    mine = exchange(profile.reshape(NDEV, 2 * particles, radial_rows), 1)
    mine = mine.reshape(NDEV, 2, particles, radial_rows)
    denoised = jnp.einsum("scpr,cst->prt", mine, table, preferred_element_type=jnp.float32)
    return denoised.astype(jnp.bfloat16)


def solution(mesh):
    placed = (
        P(("dom", "ord"), None, None),
        P("ord", None, None),
        P("ord"),
        P("ord"),
        P(),
        P("ord", None, None),
    )
    return jax.shard_map(
        on_device,
        mesh=mesh,
        in_specs=placed,
        out_specs=P(("dom", "ord"), None, None),
        check_vma=False,
    )
```

```python
import math

import jax
import jax.numpy as jnp
from jax import lax
from jax.experimental import pallas as pl
from jax.experimental.pallas import tpu as pltpu
from jax.sharding import PartitionSpec as P

NRB = 8
ITERS = 4
NZ, NY, NX = 8, 4, 4
NDOM = NZ * NY * NX
NDEV = 2 * NDOM
MESH = pl.DeviceIdType.MESH


def make_table(order_of_slot, angles):
    steps_t = jnp.arange(angles, dtype=jnp.int32)
    phase_int = order_of_slot[:, None] * steps_t[None, :] % angles
    radians = phase_int.astype(jnp.float32) * (2.0 * math.pi / angles)
    weight = math.sqrt(2.0 / angles)
    return jnp.stack([jnp.cos(radians) * weight, -jnp.sin(radians) * weight]).astype(jnp.bfloat16)


FAR_FIRST_8 = (4, 3, 5, 2, 6, 1, 7, 0)
FAR_FIRST_4 = (2, 1, 3, 0)


def dot32(a, b, dims):
    return lax.dot_general(
        a, b, (dims, ((), ())), precision=lax.Precision.HIGHEST, preferred_element_type=jnp.float32
    )


def orthonormal(image_t):
    rank, width = image_t.shape
    gram = dot32(image_t, image_t, ((1,), (1,)))
    lane_block = lax.broadcasted_iota(jnp.int32, (rank, rank * width), 1) // width
    spread = lane_block == lax.broadcasted_iota(jnp.int32, (rank, rank * width), 0)
    wide = dot32(gram, spread.astype(jnp.float32), ((1,), (0,)))
    cols = [wide[:, j * width : (j + 1) * width] for j in range(rank)]
    row_id = lax.broadcasted_iota(jnp.int32, (rank, width), 0)
    pivots = jnp.ones((rank, width), jnp.float32)
    out = image_t
    for j in range(rank):
        pivot = jnp.broadcast_to(cols[j][j : j + 1, :], (rank, width))
        pivots = jnp.where(row_id == j, pivot, pivots)
        factor = jnp.where(row_id > j, cols[j] / pivot, 0.0)
        for k in range(j + 1, rank):
            cols[k] = cols[k] - factor * cols[k][j : j + 1, :]
        out = out - factor * out[j : j + 1, :]
    return out / jnp.sqrt(pivots)


def peers():
    d = lax.axis_index("dom")
    o = lax.axis_index("ord")
    z, y, x = d // (NY * NX), (d // NX) % NY, d % NX
    at_z = [(z + k) % NZ * (NY * NX) for k in range(NZ)]
    at_y = [(y + k) % NY * NX for k in range(NY)]
    at_x = [(x + k) % NX for k in range(NX)]
    for dy in FAR_FIRST_4:
        for dx in FAR_FIRST_4:
            plane = at_y[dy] + at_x[dx]
            for dz in FAR_FIRST_8:
                for other in (True, False):
                    if other or (dz, dy, dx) != (0, 0, 0):
                        yield at_z[dz] + plane, (1 - o if other else o)


def greet_all():
    barrier = pltpu.get_barrier_semaphore()
    for pd, po in peers():
        pl.semaphore_signal(barrier, inc=1, device_id=(pd, po), device_id_type=MESH)


def exchange_blocks(src_ref, dst_ref, send_sem, recv_sem, own_sem):
    d = lax.axis_index("dom")
    o = lax.axis_index("ord")
    mine = o * NDOM + d
    own = pltpu.make_async_copy(src_ref.at[mine], dst_ref.at[mine], own_sem)
    own.start()
    pl.semaphore_wait(pltpu.get_barrier_semaphore(), NDEV - 1)
    for pd, po in peers():
        pltpu.make_async_remote_copy(
            src_ref=src_ref.at[po * NDOM + pd],
            dst_ref=dst_ref.at[mine],
            send_sem=send_sem,
            recv_sem=recv_sem,
            device_id=(pd, po),
            device_id_type=MESH,
        ).start()
    own.wait()
    most = pl.ds(0, NDEV - 1)
    everything = pltpu.make_async_remote_copy(
        src_ref=src_ref.at[most],
        dst_ref=dst_ref.at[most],
        send_sem=send_sem,
        recv_sem=recv_sem,
        device_id=(d, 1 - o),
        device_id_type=MESH,
    )
    everything.wait_send()
    everything.wait_recv()


def exchange_kernel(src_ref, dst_ref, send_sem, recv_sem, own_sem):
    greet_all()
    exchange_blocks(src_ref, dst_ref, send_sem, recv_sem, own_sem)


def profile_kernel(
    cov_ref, start_ref, masked_ref, coef_ref, dst_ref, prof_ref, send_sem, recv_sem, own_sem
):
    greet_all()
    cov = cov_ref[...]
    basis_t = start_ref[...]
    for step in range(ITERS):
        basis_t = orthonormal(dot32(basis_t, cov, ((1,), (0,))))
    eig_t = basis_t.astype(jnp.bfloat16)
    u_t = lax.dot_general(
        eig_t, masked_ref[...], (((1,), (1,)), ((), ())), preferred_element_type=jnp.float32
    ).astype(jnp.bfloat16)
    chunk = 512
    for lo in range(0, coef_ref.shape[0], chunk):
        scores = lax.dot_general(
            coef_ref[lo : lo + chunk, :],
            eig_t,
            (((1,), (1,)), ((), ())),
            preferred_element_type=jnp.float32,
        ).astype(jnp.bfloat16)
        profile = jnp.dot(scores, u_t, preferred_element_type=jnp.float32)
        blocks = profile.reshape(chunk // 8, 8, profile.shape[1]).astype(jnp.bfloat16)
        prof_ref[lo // 8 : (lo + chunk) // 8] = blocks
    exchange_blocks(prof_ref, dst_ref, send_sem, recv_sem, own_sem)


def comm_call(kernel, collective_id, shape, *operands, scratch=(), name):
    vmem = pl.BlockSpec(memory_space=pltpu.VMEM)
    return pl.pallas_call(
        kernel,
        out_shape=jax.ShapeDtypeStruct(shape, jnp.bfloat16),
        in_specs=[vmem] * len(operands),
        out_specs=vmem,
        scratch_shapes=[*scratch, *[pltpu.SemaphoreType.DMA] * 3],
        compiler_params=pltpu.CompilerParams(collective_id=collective_id, has_side_effects=True),
        name=name,
    )(*operands)


def on_device(polar_images, radial_basis, radial_start, radial_count, order_of_slot, start_block):
    particles, radial_rows, angles = polar_images.shape
    table = make_table(order_of_slot, angles)
    spectrum = jnp.einsum(
        "cst,prt->scpr", table, polar_images, preferred_element_type=jnp.float32
    ).astype(jnp.bfloat16)
    shape = (NDEV, 2 * particles, radial_rows)
    rows = comm_call(exchange_kernel, 0, shape, spectrum.reshape(shape), name="spectra")
    rows = rows.reshape(NDEV * 2 * particles, radial_rows)

    slot = lax.axis_index("dom")
    basis = lax.dynamic_index_in_dim(radial_basis, slot, 0, keepdims=False)
    first_row = lax.dynamic_index_in_dim(radial_start, slot, 0, keepdims=False) * (radial_rows // NRB)
    count = lax.dynamic_index_in_dim(radial_count, slot, 0, keepdims=False)
    start_t = lax.dynamic_index_in_dim(start_block, slot, 0, keepdims=False)
    keep_rows = jnp.arange(radial_rows)[:, None] >= first_row
    keep_cols = jnp.arange(basis.shape[1])[None, :] < count
    masked = jnp.where(keep_rows & keep_cols, basis, jnp.zeros_like(basis))

    coef = jnp.dot(rows, masked, preferred_element_type=jnp.float32).astype(jnp.bfloat16)
    cov = jnp.einsum("nq,nm->qm", coef, coef, preferred_element_type=jnp.float32)
    mine = comm_call(
        profile_kernel,
        1,
        shape,
        cov,
        start_t,
        masked,
        coef,
        scratch=[pltpu.VMEM(shape, jnp.bfloat16)],
        name="profiles",
    )
    mine = mine.reshape(NDEV, 2, particles, radial_rows)
    denoised = jnp.einsum("scpr,cst->prt", mine, table, preferred_element_type=jnp.float32)
    return denoised.astype(jnp.bfloat16)


def solution(mesh):
    placed = (
        P(("dom", "ord"), None, None),
        P("ord", None, None),
        P("ord"),
        P("ord"),
        P(),
        P("ord", None, None),
    )
    return jax.shard_map(
        on_device,
        mesh=mesh,
        in_specs=placed,
        out_specs=P(("dom", "ord"), None, None),
        check_vma=False,
    )
```

```python
import math

import jax
import jax.numpy as jnp
from jax import lax
from jax.experimental import pallas as pl
from jax.experimental.pallas import tpu as pltpu
from jax.sharding import PartitionSpec as P

NRB = 8
ITERS = 4
NZ, NY, NX = 8, 4, 4
NDOM = NZ * NY * NX
NDEV = 2 * NDOM
MESH = pl.DeviceIdType.MESH


FAR_FIRST_8 = (4, 3, 5, 2, 6, 1, 7, 0)
FAR_FIRST_4 = (2, 1, 3, 0)


def dot32(a, b, dims):
    return lax.dot_general(
        a, b, (dims, ((), ())), precision=lax.Precision.HIGHEST, preferred_element_type=jnp.float32
    )


def orthonormal(image_t):
    rank, width = image_t.shape
    gram = dot32(image_t, image_t, ((1,), (1,)))
    lane_block = lax.broadcasted_iota(jnp.int32, (rank, rank * width), 1) // width
    spread = lane_block == lax.broadcasted_iota(jnp.int32, (rank, rank * width), 0)
    wide = dot32(gram, spread.astype(jnp.float32), ((1,), (0,)))
    cols = [wide[:, j * width : (j + 1) * width] for j in range(rank)]
    row_id = lax.broadcasted_iota(jnp.int32, (rank, width), 0)
    pivots = jnp.ones((rank, width), jnp.float32)
    out = image_t
    for j in range(rank):
        pivot = jnp.broadcast_to(cols[j][j : j + 1, :], (rank, width))
        pivots = jnp.where(row_id == j, pivot, pivots)
        factor = jnp.where(row_id > j, cols[j] / pivot, 0.0)
        for k in range(j + 1, rank):
            cols[k] = cols[k] - factor * cols[k][j : j + 1, :]
        out = out - factor * out[j : j + 1, :]
    return out / jnp.sqrt(pivots)


def peers():
    d = lax.axis_index("dom")
    o = lax.axis_index("ord")
    z, y, x = d // (NY * NX), (d // NX) % NY, d % NX
    at_z = [(z + k) % NZ * (NY * NX) for k in range(NZ)]
    at_y = [(y + k) % NY * NX for k in range(NY)]
    at_x = [(x + k) % NX for k in range(NX)]
    for dy in FAR_FIRST_4:
        for dx in FAR_FIRST_4:
            plane = at_y[dy] + at_x[dx]
            for dz in FAR_FIRST_8:
                for other in (True, False):
                    if other or (dz, dy, dx) != (0, 0, 0):
                        yield at_z[dz] + plane, (1 - o if other else o)


def greet_all():
    barrier = pltpu.get_barrier_semaphore()
    for pd, po in peers():
        pl.semaphore_signal(barrier, inc=1, device_id=(pd, po), device_id_type=MESH)


def exchange_blocks(src_ref, dst_ref, send_sem, recv_sem, own_sem):
    d = lax.axis_index("dom")
    o = lax.axis_index("ord")
    mine = o * NDOM + d
    own = pltpu.make_async_copy(src_ref.at[mine], dst_ref.at[mine], own_sem)
    own.start()
    for pd, po in peers():
        pltpu.make_async_remote_copy(
            src_ref=src_ref.at[po * NDOM + pd],
            dst_ref=dst_ref.at[mine],
            send_sem=send_sem,
            recv_sem=recv_sem,
            device_id=(pd, po),
            device_id_type=MESH,
        ).start()
    own.wait()
    most = pl.ds(0, NDEV - 1)
    everything = pltpu.make_async_remote_copy(
        src_ref=src_ref.at[most],
        dst_ref=dst_ref.at[most],
        send_sem=send_sem,
        recv_sem=recv_sem,
        device_id=(d, 1 - o),
        device_id_type=MESH,
    )
    everything.wait_send()
    everything.wait_recv()


def fill_table(order_ref, table_ref):
    angles = table_ref.shape[1]
    weight = math.sqrt(2.0 / angles)
    for half in range(2):
        row = order_ref[half : half + 1, :].astype(jnp.float32)
        k = jnp.broadcast_to(row, (128, 128)).T.astype(jnp.int32)
        lane = lax.broadcasted_iota(jnp.int32, (128, 128), 1)
        turn = (k * lane) & (angles - 1)
        quarter = (turn + angles // 8) >> 7
        angle = (turn - quarter * (angles // 4)).astype(jnp.float32) * (2.0 * math.pi / angles)
        sq = angle * angle
        cos = 1.0 + sq * (-1 / 2 + sq * (1 / 24 + sq * (-1 / 720 + sq * (1 / 40320))))
        sin = angle * (1.0 + sq * (-1 / 6 + sq * (1 / 120 + sq * (-1 / 5040 + sq * (1 / 362880)))))
        cos = cos * weight
        sin = sin * weight
        for b in range(angles // 128):
            quadrant = (quarter + b * k) & 3
            odd = (quadrant & 1) == 1
            upper = quadrant >= 2
            even_sign = jnp.where(upper, -1.0, 1.0)
            real = jnp.where(odd, -sin, cos) * even_sign
            imag = jnp.where(odd, -cos, -sin) * even_sign
            span = slice(128 * b, 128 * (b + 1))
            table_ref[128 * half : 128 * (half + 1), span] = real.astype(jnp.bfloat16)
            table_ref[256 + 128 * half : 256 + 128 * (half + 1), span] = imag.astype(jnp.bfloat16)


def fill_spectrum(table_ref, images_ref, wide_ref, spec_ref):
    for p in range(images_ref.shape[0]):
        for c in range(2):
            part = lax.dot_general(
                table_ref[256 * c : 256 * (c + 1), :],
                images_ref[p],
                (((1,), (1,)), ((), ())),
                preferred_element_type=jnp.float32,
            )
            wide_ref[pl.ds(4 * c + p, NDEV, stride=8), :] = part
    spec_ref[...] = wide_ref[...].reshape(spec_ref.shape).astype(jnp.bfloat16)


def whole_kernel(
    images_ref,
    radial_ref,
    first_ref,
    count_ref,
    order_ref,
    start_ref,
    table_ref,
    out_ref,
    wide_ref,
    spec_ref,
    rows_ref,
    coef_ref,
    prof_ref,
    radial_own,
    start_own,
    send_1,
    recv_1,
    own_1,
    send_2,
    recv_2,
    own_2,
    load_1,
    load_2,
):
    slot = lax.axis_index("dom")
    greet_all()
    radial_load = pltpu.make_async_copy(radial_ref.at[slot], radial_own, load_1)
    start_load = pltpu.make_async_copy(start_ref.at[slot], start_own, load_2)
    radial_load.start()
    start_load.start()
    fill_table(order_ref, table_ref)
    fill_spectrum(table_ref, images_ref, wide_ref, spec_ref)
    radial_load.wait()
    start_load.wait()
    first_row = first_ref[slot] * (radial_own.shape[0] // NRB)
    row_id = lax.broadcasted_iota(jnp.int32, radial_own.shape, 0)
    col_id = lax.broadcasted_iota(jnp.int32, radial_own.shape, 1)
    keep = (row_id >= first_row) & (col_id < count_ref[slot])
    masked = jnp.where(keep, radial_own[...].astype(jnp.float32), 0.0).astype(jnp.bfloat16)
    pl.semaphore_wait(pltpu.get_barrier_semaphore(), NDEV - 1)
    exchange_blocks(spec_ref, rows_ref, send_1, recv_1, own_1)

    chunk = 512
    cov = jnp.zeros((masked.shape[1], masked.shape[1]), jnp.float32)
    for lo in range(0, coef_ref.shape[0], chunk):
        block = rows_ref[lo // 8 : (lo + chunk) // 8].astype(jnp.float32)
        rows = block.reshape(chunk, block.shape[2]).astype(jnp.bfloat16)
        coef = jnp.dot(rows, masked, preferred_element_type=jnp.float32).astype(jnp.bfloat16)
        coef_ref[lo : lo + chunk, :] = coef
        cov = cov + lax.dot_general(
            coef, coef, (((0,), (0,)), ((), ())), preferred_element_type=jnp.float32
        )
    basis_t = start_own[...]
    for step in range(ITERS):
        basis_t = orthonormal(dot32(basis_t, cov, ((1,), (0,))))
    eig_t = basis_t.astype(jnp.bfloat16)
    u_t = lax.dot_general(
        eig_t, masked, (((1,), (1,)), ((), ())), preferred_element_type=jnp.float32
    ).astype(jnp.bfloat16)
    for lo in range(0, coef_ref.shape[0], chunk):
        scores = lax.dot_general(
            coef_ref[lo : lo + chunk, :],
            eig_t,
            (((1,), (1,)), ((), ())),
            preferred_element_type=jnp.float32,
        ).astype(jnp.bfloat16)
        profile = jnp.dot(scores, u_t, preferred_element_type=jnp.float32)
        blocks = profile.reshape(chunk // 8, 8, profile.shape[1]).astype(jnp.bfloat16)
        prof_ref[lo // 8 : (lo + chunk) // 8] = blocks
    exchange_blocks(prof_ref, out_ref, send_2, recv_2, own_2)


def on_device(polar_images, radial_basis, radial_start, radial_count, order_of_slot, start_block):
    particles, radial_rows, angles = polar_images.shape
    rank, width = start_block.shape[1:]
    slots = order_of_slot.shape[0]
    shape = (NDEV, 2 * particles, radial_rows)
    vmem = pl.BlockSpec(memory_space=pltpu.VMEM)
    smem = pl.BlockSpec(memory_space=pltpu.SMEM)
    anywhere = pl.BlockSpec(memory_space=pl.ANY)
    dma = pltpu.SemaphoreType.DMA
    table, mine = pl.pallas_call(
        whole_kernel,
        out_shape=(
            jax.ShapeDtypeStruct((2 * slots, angles), jnp.bfloat16),
            jax.ShapeDtypeStruct(shape, jnp.bfloat16),
        ),
        in_specs=[vmem, anywhere, smem, smem, vmem, anywhere],
        out_specs=(vmem, vmem),
        scratch_shapes=[
            pltpu.VMEM((NDEV * 2 * particles, radial_rows), jnp.float32),
            pltpu.VMEM(shape, jnp.bfloat16),
            pltpu.VMEM(shape, jnp.bfloat16),
            pltpu.VMEM((NDEV * 2 * particles, width), jnp.bfloat16),
            pltpu.VMEM(shape, jnp.bfloat16),
            pltpu.VMEM(radial_basis.shape[1:], jnp.bfloat16),
            pltpu.VMEM((rank, width), jnp.float32),
            *[dma] * 8,
        ],
        compiler_params=pltpu.CompilerParams(collective_id=0, has_side_effects=True),
        name="whole",
    )(
        polar_images,
        radial_basis,
        radial_start,
        radial_count,
        order_of_slot.reshape(2, slots // 2),
        start_block,
    )
    mine = mine.reshape(NDEV, 2, particles, radial_rows)
    table = table.reshape(2, slots, angles)
    denoised = jnp.einsum("scpr,cst->prt", mine, table, preferred_element_type=jnp.float32)
    return denoised.astype(jnp.bfloat16)


def solution(mesh):
    placed = (
        P(("dom", "ord"), None, None),
        P("ord", None, None),
        P("ord"),
        P("ord"),
        P(),
        P("ord", None, None),
    )
    return jax.shard_map(
        on_device,
        mesh=mesh,
        in_specs=placed,
        out_specs=P(("dom", "ord"), None, None),
        check_vma=False,
    )
```

```python
import math

import jax
import jax.numpy as jnp
from jax import lax
from jax.experimental import pallas as pl
from jax.experimental.pallas import tpu as pltpu
from jax.sharding import PartitionSpec as P

NRB = 8
ITERS = 4
NZ, NY, NX = 8, 4, 4
NDOM = NZ * NY * NX
NDEV = 2 * NDOM
MESH = pl.DeviceIdType.MESH


FAR_FIRST_8 = (4, 3, 5, 2, 6, 1, 7, 0)
FAR_FIRST_4 = (2, 1, 3, 0)


def dot32(a, b, dims):
    return lax.dot_general(
        a, b, (dims, ((), ())), precision=lax.Precision.HIGHEST, preferred_element_type=jnp.float32
    )


def orthonormal(image_t):
    rank, width = image_t.shape
    gram = dot32(image_t, image_t, ((1,), (1,)))
    lane_block = lax.broadcasted_iota(jnp.int32, (rank, rank * width), 1) // width
    spread = lane_block == lax.broadcasted_iota(jnp.int32, (rank, rank * width), 0)
    wide = dot32(gram, spread.astype(jnp.float32), ((1,), (0,)))
    cols = [wide[:, j * width : (j + 1) * width] for j in range(rank)]
    row_id = lax.broadcasted_iota(jnp.int32, (rank, width), 0)
    pivots = jnp.ones((rank, width), jnp.float32)
    out = image_t
    for j in range(rank):
        pivot = jnp.broadcast_to(cols[j][j : j + 1, :], (rank, width))
        pivots = jnp.where(row_id == j, pivot, pivots)
        factor = jnp.where(row_id > j, cols[j] / pivot, 0.0)
        for k in range(j + 1, rank):
            cols[k] = cols[k] - factor * cols[k][j : j + 1, :]
        out = out - factor * out[j : j + 1, :]
    return out / jnp.sqrt(pivots)


def place():
    d = lax.axis_index("dom")
    return d, lax.axis_index("ord"), d // (NY * NX), (d // NX) % NY, d % NX


def line_peers(axis):
    d, o, z, y, x = place()
    if axis == "z":
        return [((z + k) % NZ * (NY * NX) + y * NX + x, o) for k in range(1, NZ)]
    if axis == "y":
        return [(z * (NY * NX) + (y + k) % NY * NX + x, o) for k in range(1, NY)]
    return [(d - x + (x + k) % NX, o) for k in range(1, NX)]


def same_core(x_offsets):
    d, o, z, y, x = place()
    at_z = [(z + k) % NZ * (NY * NX) for k in range(NZ)]
    at_y = [(y + k) % NY * NX for k in range(NY)]
    at_x = [(x + k) % NX for k in range(NX)]
    for dx in x_offsets:
        for dy in FAR_FIRST_4:
            plane = at_y[dy] + at_x[dx]
            for dz in FAR_FIRST_8:
                if (dz, dy, dx) != (0, 0, 0):
                    yield at_z[dz] + plane


def greet(semaphore, devices):
    for device in devices:
        pl.semaphore_signal(semaphore, inc=1, device_id=device, device_id_type=MESH)


def send_blocks(src_ref, dst_ref, send_sem, recv_sem, targets):
    d, o = place()[:2]
    for pd in targets:
        pltpu.make_async_remote_copy(
            src_ref=src_ref.at[pd],
            dst_ref=dst_ref.at[d],
            send_sem=send_sem,
            recv_sem=recv_sem,
            device_id=(pd, o),
            device_id_type=MESH,
        ).start()


def wait_blocks(src_ref, dst_ref, send_sem, recv_sem):
    d, o = place()[:2]
    most = pl.ds(0, NDOM - 1)
    everything = pltpu.make_async_remote_copy(
        src_ref=src_ref.at[most],
        dst_ref=dst_ref.at[most],
        send_sem=send_sem,
        recv_sem=recv_sem,
        device_id=(d, 1 - o),
        device_id_type=MESH,
    )
    everything.wait_send()
    everything.wait_recv()


def to_sibling(src_ref, dst_ref, send_sem, recv_sem):
    d, o = place()[:2]
    return pltpu.make_async_remote_copy(
        src_ref=src_ref,
        dst_ref=dst_ref,
        send_sem=send_sem,
        recv_sem=recv_sem,
        device_id=(d, 1 - o),
        device_id_type=MESH,
    )


def fill_table(order_ref, table_ref):
    angles = table_ref.shape[1]
    weight = math.sqrt(2.0 / angles)
    for half in range(2):
        row = order_ref[half : half + 1, :].astype(jnp.float32)
        k = jnp.broadcast_to(row, (128, 128)).T.astype(jnp.int32)
        lane = lax.broadcasted_iota(jnp.int32, (128, 128), 1)
        turn = (k * lane) & (angles - 1)
        quarter = (turn + angles // 8) >> 7
        angle = (turn - quarter * (angles // 4)).astype(jnp.float32) * (2.0 * math.pi / angles)
        sq = angle * angle
        cos = 1.0 + sq * (-1 / 2 + sq * (1 / 24 + sq * (-1 / 720 + sq * (1 / 40320))))
        sin = angle * (1.0 + sq * (-1 / 6 + sq * (1 / 120 + sq * (-1 / 5040 + sq * (1 / 362880)))))
        cos = cos * weight
        sin = sin * weight
        for b in range(angles // 128):
            quadrant = (quarter + b * k) & 3
            odd = (quadrant & 1) == 1
            upper = quadrant >= 2
            even_sign = jnp.where(upper, -1.0, 1.0)
            real = jnp.where(odd, -sin, cos) * even_sign
            imag = jnp.where(odd, -cos, -sin) * even_sign
            span = slice(128 * b, 128 * (b + 1))
            table_ref[128 * half : 128 * (half + 1), span] = real.astype(jnp.bfloat16)
            table_ref[256 + 128 * half : 256 + 128 * (half + 1), span] = imag.astype(jnp.bfloat16)


def fill_spectrum(table_ref, images_ref, wide_ref):
    slots = table_ref.shape[0] // 2
    for p in range(0, images_ref.shape[0], 2):
        pair = images_ref[p : p + 2].reshape(2 * images_ref.shape[1], images_ref.shape[2])
        for c in range(2):
            part = lax.dot_general(
                table_ref[slots * c : slots * (c + 1), :],
                pair,
                (((1,), (1,)), ((), ())),
                preferred_element_type=jnp.float32,
            )
            wide_ref[pl.ds(4 * c + p, slots, stride=8), :] = part[:, :128]
            wide_ref[pl.ds(4 * c + p + 1, slots, stride=8), :] = part[:, 128:]


def whole_kernel(
    images_ref,
    radial_ref,
    first_ref,
    count_ref,
    order_ref,
    start_ref,
    table_ref,
    out_ref,
    wide_ref,
    away_ref,
    spec_ref,
    rows_ref,
    coef_ref,
    prof_ref,
    back_ref,
    radial_own,
    start_own,
    send_0,
    recv_0,
    send_1,
    recv_1,
    own_1,
    send_2,
    recv_2,
    own_2,
    send_3,
    recv_3,
    own_3,
    load_1,
    load_2,
    sem_y,
    sem_x,
):
    slot, core = place()[:2]
    barrier = pltpu.get_barrier_semaphore()
    greet(barrier, line_peers("z") + line_peers("y") + line_peers("x") + [(slot, 1 - core)])
    radial_load = pltpu.make_async_copy(radial_ref.at[slot], radial_own, load_1)
    start_load = pltpu.make_async_copy(start_ref.at[slot], start_own, load_2)
    radial_load.start()
    start_load.start()
    fill_table(order_ref, table_ref)
    fill_spectrum(table_ref, images_ref, wide_ref)
    half = NDOM * 8
    away = wide_ref[pl.ds((1 - core) * half, half), :]
    away_ref[...] = away.reshape(away_ref.shape).astype(jnp.bfloat16)
    kept = wide_ref[pl.ds(core * half, half), :]
    spec_ref[:, pl.ds(core, 1)] = kept.reshape(NDOM, 1, 8, kept.shape[1]).astype(jnp.bfloat16)

    pl.semaphore_wait(barrier, NZ + NY + NX - 2)
    greet(sem_y, line_peers("y"))
    swap = to_sibling(away_ref, spec_ref.at[:, core], send_0, recv_0)
    swap.start()
    radial_load.wait()
    start_load.wait()
    first_row = first_ref[slot] * (radial_own.shape[0] // NRB)
    row_id = lax.broadcasted_iota(jnp.int32, radial_own.shape, 0)
    col_id = lax.broadcasted_iota(jnp.int32, radial_own.shape, 1)
    keep = (row_id >= first_row) & (col_id < count_ref[slot])
    masked = jnp.where(keep, radial_own[...].astype(jnp.float32), 0.0).astype(jnp.bfloat16)
    pl.semaphore_wait(sem_y, NY - 1)
    greet(sem_x, line_peers("x"))
    swap.wait()
    own = pltpu.make_async_copy(spec_ref.at[slot], rows_ref.at[slot], own_1)
    own.start()
    send_blocks(spec_ref, rows_ref, send_1, recv_1, same_core((0,)))
    pl.semaphore_wait(sem_x, NX - 1)
    send_blocks(spec_ref, rows_ref, send_1, recv_1, same_core((2, 1, 3)))
    own.wait()
    wait_blocks(spec_ref, rows_ref, send_1, recv_1)

    chunk = 512
    cov = jnp.zeros((masked.shape[1], masked.shape[1]), jnp.float32)
    for lo in range(0, coef_ref.shape[0], chunk):
        block = rows_ref[lo // 16 : (lo + chunk) // 16].astype(jnp.float32)
        rows = block.reshape(chunk, block.shape[3]).astype(jnp.bfloat16)
        coef = jnp.dot(rows, masked, preferred_element_type=jnp.float32).astype(jnp.bfloat16)
        coef_ref[lo : lo + chunk, :] = coef
        cov = cov + lax.dot_general(
            coef, coef, (((0,), (0,)), ((), ())), preferred_element_type=jnp.float32
        )
    basis_t = start_own[...]
    for step in range(ITERS):
        basis_t = orthonormal(dot32(basis_t, cov, ((1,), (0,))))
    eig_t = basis_t.astype(jnp.bfloat16)
    u_t = lax.dot_general(
        eig_t, masked, (((1,), (1,)), ((), ())), preferred_element_type=jnp.float32
    ).astype(jnp.bfloat16)
    for lo in range(0, coef_ref.shape[0], chunk):
        scores = lax.dot_general(
            coef_ref[lo : lo + chunk, :],
            eig_t,
            (((1,), (1,)), ((), ())),
            preferred_element_type=jnp.float32,
        ).astype(jnp.bfloat16)
        profile = jnp.dot(scores, u_t, preferred_element_type=jnp.float32)
        blocks = profile.reshape(chunk // 16, 2, 8, profile.shape[1]).astype(jnp.bfloat16)
        prof_ref[lo // 16 : (lo + chunk) // 16] = blocks
    own = pltpu.make_async_copy(prof_ref.at[slot], back_ref.at[slot], own_2)
    own.start()
    send_blocks(prof_ref, back_ref, send_2, recv_2, same_core((2, 1, 3, 0)))
    own.wait()
    wait_blocks(prof_ref, back_ref, send_2, recv_2)

    swap = to_sibling(back_ref.at[:, 1 - core], out_ref.at[core], send_3, recv_3)
    swap.start()
    own = pltpu.make_async_copy(back_ref.at[:, core], out_ref.at[core], own_3)
    own.start()
    swap.wait()
    own.wait()


def on_device(polar_images, radial_basis, radial_start, radial_count, order_of_slot, start_block):
    particles, radial_rows, angles = polar_images.shape
    rank, width = start_block.shape[1:]
    slots = order_of_slot.shape[0]
    blocks = (NDOM, 2, 2 * particles, radial_rows)
    vmem = pl.BlockSpec(memory_space=pltpu.VMEM)
    smem = pl.BlockSpec(memory_space=pltpu.SMEM)
    anywhere = pl.BlockSpec(memory_space=pl.ANY)
    dma = pltpu.SemaphoreType.DMA
    table, mine = pl.pallas_call(
        whole_kernel,
        out_shape=(
            jax.ShapeDtypeStruct((2 * slots, angles), jnp.bfloat16),
            jax.ShapeDtypeStruct((2, NDOM, 2 * particles, radial_rows), jnp.bfloat16),
        ),
        in_specs=[vmem, anywhere, smem, smem, vmem, anywhere],
        out_specs=(vmem, vmem),
        scratch_shapes=[
            pltpu.VMEM((NDEV * 2 * particles, radial_rows), jnp.float32),
            pltpu.VMEM((NDOM, 2 * particles, radial_rows), jnp.bfloat16),
            pltpu.VMEM(blocks, jnp.bfloat16),
            pltpu.VMEM(blocks, jnp.bfloat16),
            pltpu.VMEM((NDEV * 2 * particles, width), jnp.bfloat16),
            pltpu.VMEM(blocks, jnp.bfloat16),
            pltpu.VMEM(blocks, jnp.bfloat16),
            pltpu.VMEM(radial_basis.shape[1:], jnp.bfloat16),
            pltpu.VMEM((rank, width), jnp.float32),
            *[dma] * 13,
            *[pltpu.SemaphoreType.REGULAR] * 2,
        ],
        compiler_params=pltpu.CompilerParams(collective_id=0, has_side_effects=True),
        name="whole",
    )(
        polar_images,
        radial_basis,
        radial_start,
        radial_count,
        order_of_slot.reshape(2, slots // 2),
        start_block,
    )
    mine = mine.reshape(NDEV, 2, particles, radial_rows)
    table = table.reshape(2, slots, angles)
    denoised = jnp.einsum("scpr,cst->prt", mine, table, preferred_element_type=jnp.float32)
    return denoised.astype(jnp.bfloat16)


def solution(mesh):
    placed = (
        P(("dom", "ord"), None, None),
        P("ord", None, None),
        P("ord"),
        P("ord"),
        P(),
        P("ord", None, None),
    )
    return jax.shard_map(
        on_device,
        mesh=mesh,
        in_specs=placed,
        out_specs=P(("dom", "ord"), None, None),
        check_vma=False,
    )
```

```python
import math

import jax
import jax.numpy as jnp
from jax import lax
from jax.experimental import pallas as pl
from jax.experimental.pallas import tpu as pltpu
from jax.sharding import PartitionSpec as P

NRB = 8
ITERS = 4
NZ, NY, NX = 8, 4, 4
NDOM = NZ * NY * NX
NPLANE = 2 * NY * NX
MESH = pl.DeviceIdType.MESH


FAR_FIRST_8 = (4, 3, 5, 2, 6, 1, 7, 0)
FAR_FIRST_4 = (2, 1, 3, 0)


def dot32(a, b, dims):
    return lax.dot_general(
        a, b, (dims, ((), ())), precision=lax.Precision.HIGHEST, preferred_element_type=jnp.float32
    )


def orthonormal(image_t):
    rank, width = image_t.shape
    gram = dot32(image_t, image_t, ((1,), (1,)))
    lane_block = lax.broadcasted_iota(jnp.int32, (rank, rank * width), 1) // width
    spread = lane_block == lax.broadcasted_iota(jnp.int32, (rank, rank * width), 0)
    wide = dot32(gram, spread.astype(jnp.float32), ((1,), (0,)))
    cols = [wide[:, j * width : (j + 1) * width] for j in range(rank)]
    row_id = lax.broadcasted_iota(jnp.int32, (rank, width), 0)
    pivots = jnp.ones((rank, width), jnp.float32)
    out = image_t
    for j in range(rank):
        pivot = jnp.broadcast_to(cols[j][j : j + 1, :], (rank, width))
        pivots = jnp.where(row_id == j, pivot, pivots)
        factor = jnp.where(row_id > j, cols[j] / pivot, 0.0)
        for k in range(j + 1, rank):
            cols[k] = cols[k] - factor * cols[k][j : j + 1, :]
        out = out - factor * out[j : j + 1, :]
    return out / jnp.sqrt(pivots)


def place():
    d = lax.axis_index("dom")
    return d, lax.axis_index("ord"), d // (NY * NX), (d // NX) % NY, d % NX


def z_peers():
    d, o, z, y, x = place()
    for k in FAR_FIRST_8[:-1]:
        pz = (z + k) % NZ
        yield pz, pz * (NY * NX) + y * NX + x


def plane_peers():
    d, o, z, y, x = place()
    at_y = [(y + k) % NY * NX for k in range(NY)]
    at_x = [(x + k) % NX for k in range(NX)]
    for dy in FAR_FIRST_4:
        for dx in FAR_FIRST_4:
            m = at_y[dy] + at_x[dx]
            for po in (1 - o, o) if (dy, dx) != (0, 0) else (1 - o,):
                yield po * (NY * NX) + m, z * (NY * NX) + m, po


def remote(src_ref, dst_ref, send_sem, recv_sem, device):
    return pltpu.make_async_remote_copy(
        src_ref=src_ref,
        dst_ref=dst_ref,
        send_sem=send_sem,
        recv_sem=recv_sem,
        device_id=device,
        device_id_type=MESH,
    )


def wait_blocks(src_ref, dst_ref, send_sem, recv_sem, blocks):
    d, o = place()[:2]
    most = pl.ds(0, blocks)
    everything = remote(src_ref.at[most], dst_ref.at[most], send_sem, recv_sem, (d, 1 - o))
    everything.wait_send()
    everything.wait_recv()


def plane_exchange(src_ref, dst_ref, send_sem, recv_sem, own_sem):
    d, o, z, y, x = place()
    mine = o * (NY * NX) + y * NX + x
    for index, pd, po in plane_peers():
        remote(src_ref.at[index], dst_ref.at[mine], send_sem, recv_sem, (pd, po)).start()
    own = pltpu.make_async_copy(src_ref.at[mine], dst_ref.at[mine], own_sem)
    own.start()
    own.wait()
    wait_blocks(src_ref, dst_ref, send_sem, recv_sem, NPLANE - 1)


def fill_table(order_ref, table_ref):
    angles = table_ref.shape[1]
    weight = math.sqrt(2.0 / angles)
    for half in range(2):
        row = order_ref[half : half + 1, :].astype(jnp.float32)
        k = jnp.broadcast_to(row, (128, 128)).T.astype(jnp.int32)
        lane = lax.broadcasted_iota(jnp.int32, (128, 128), 1)
        turn = (k * lane) & (angles - 1)
        quarter = (turn + angles // 8) >> 7
        angle = (turn - quarter * (angles // 4)).astype(jnp.float32) * (2.0 * math.pi / angles)
        sq = angle * angle
        cos = 1.0 + sq * (-1 / 2 + sq * (1 / 24 + sq * (-1 / 720 + sq * (1 / 40320))))
        sin = angle * (1.0 + sq * (-1 / 6 + sq * (1 / 120 + sq * (-1 / 5040 + sq * (1 / 362880)))))
        cos = cos * weight
        sin = sin * weight
        for b in range(angles // 128):
            quadrant = (quarter + b * k) & 3
            odd = (quadrant & 1) == 1
            upper = quadrant >= 2
            even_sign = jnp.where(upper, -1.0, 1.0)
            real = jnp.where(odd, -sin, cos) * even_sign
            imag = jnp.where(odd, -cos, -sin) * even_sign
            span = slice(128 * b, 128 * (b + 1))
            table_ref[128 * half : 128 * (half + 1), span] = real.astype(jnp.bfloat16)
            table_ref[256 + 128 * half : 256 + 128 * (half + 1), span] = imag.astype(jnp.bfloat16)


def fill_spectrum(table_ref, images_ref, wide_ref):
    slots = table_ref.shape[0] // 2
    for p in range(0, images_ref.shape[0], 2):
        pair = images_ref[p : p + 2].reshape(2 * images_ref.shape[1], images_ref.shape[2])
        for c in range(2):
            part = lax.dot_general(
                table_ref[slots * c : slots * (c + 1), :],
                pair,
                (((1,), (1,)), ((), ())),
                preferred_element_type=jnp.float32,
            )
            wide_ref[pl.ds(4 * c + p, slots, stride=8), :] = part[:, :128]
            wide_ref[pl.ds(4 * c + p + 1, slots, stride=8), :] = part[:, 128:]


def whole_kernel(
    images_ref,
    radial_ref,
    first_ref,
    count_ref,
    order_ref,
    start_ref,
    table_ref,
    out_ref,
    wide_ref,
    spec_ref,
    rows_ref,
    masked_ref,
    coef_ref,
    part_ref,
    given_ref,
    taken_ref,
    eig_ref,
    eigs_ref,
    prof_ref,
    start_own,
    send_1,
    recv_1,
    own_1,
    send_2,
    recv_2,
    send_3,
    recv_3,
    send_4,
    recv_4,
    own_4,
    load_1,
    load_2,
):
    d, o, z, y, x = place()
    first_slot = (y * NX + x) * NZ
    barrier = pltpu.get_barrier_semaphore()
    for _, pd in z_peers():
        pl.semaphore_signal(barrier, inc=1, device_id=(pd, o), device_id_type=MESH)
    for _, pd, po in plane_peers():
        pl.semaphore_signal(barrier, inc=1, device_id=(pd, po), device_id_type=MESH)
    radial_load = pltpu.make_async_copy(radial_ref.at[pl.ds(first_slot, NZ)], masked_ref, load_1)
    start_load = pltpu.make_async_copy(start_ref.at[first_slot + z], start_own, load_2)
    radial_load.start()
    start_load.start()
    fill_table(order_ref, table_ref)
    fill_spectrum(table_ref, images_ref, wide_ref)
    spec_ref[...] = wide_ref[...].reshape(spec_ref.shape).astype(jnp.bfloat16)
    radial_load.wait()
    start_load.wait()
    radial_rows, width = masked_ref.shape[1:]
    row_id = lax.broadcasted_iota(jnp.int32, (radial_rows, width), 0)
    col_id = lax.broadcasted_iota(jnp.int32, (radial_rows, width), 1)
    for j in range(NZ):
        first_row = first_ref[first_slot + j] * (radial_rows // NRB)
        keep = (row_id >= first_row) & (col_id < count_ref[first_slot + j])
        masked = jnp.where(keep, masked_ref[j].astype(jnp.float32), 0.0)
        masked_ref[j] = masked.astype(jnp.bfloat16)
    pl.semaphore_wait(barrier, NPLANE - 1 + NZ - 1)
    plane_exchange(spec_ref, rows_ref, send_1, recv_1, own_1)

    waiting = None
    for j, pd in [*z_peers(), (z, None)]:
        rows = rows_ref[:, j].astype(jnp.float32).reshape(NPLANE * 8, radial_rows).astype(jnp.bfloat16)
        coef = jnp.dot(rows, masked_ref[j], preferred_element_type=jnp.float32).astype(jnp.bfloat16)
        coef_ref[j] = coef
        part = lax.dot_general(
            coef, coef, (((0,), (0,)), ((), ())), preferred_element_type=jnp.float32
        )
        if pd is not None:
            given_ref[j] = part.astype(jnp.bfloat16)
        if waiting is not None:
            waiting.start()
        if pd is not None:
            waiting = remote(given_ref.at[j], taken_ref.at[z], send_2, recv_2, (pd, o))
    part_ref[...] = part
    wait_blocks(given_ref, taken_ref, send_2, recv_2, NZ - 1)
    cov = part_ref[...]
    for k in range(1, NZ):
        cov = cov + taken_ref[(z + k) % NZ].astype(jnp.float32)

    basis_t = start_own[...]
    for step in range(ITERS):
        basis_t = orthonormal(dot32(basis_t, cov, ((1,), (0,))))
    eig_t = basis_t.astype(jnp.bfloat16)
    eig_ref[...] = eig_t
    eigs_ref[z] = eig_t
    for _, pd in z_peers():
        remote(eig_ref, eigs_ref.at[z], send_3, recv_3, (pd, o)).start()
    wait_blocks(eigs_ref, eigs_ref, send_3, recv_3, NZ - 1)

    for j in range(NZ):
        eig_t = eigs_ref[j]
        u_t = lax.dot_general(
            eig_t, masked_ref[j], (((1,), (1,)), ((), ())), preferred_element_type=jnp.float32
        ).astype(jnp.bfloat16)
        scores = lax.dot_general(
            coef_ref[j], eig_t, (((1,), (1,)), ((), ())), preferred_element_type=jnp.float32
        ).astype(jnp.bfloat16)
        profile = jnp.dot(scores, u_t, preferred_element_type=jnp.float32)
        prof_ref[:, j] = profile.reshape(NPLANE, 8, radial_rows).astype(jnp.bfloat16)
    plane_exchange(prof_ref, out_ref, send_4, recv_4, own_4)


def on_device(polar_images, radial_basis, radial_start, radial_count, order_of_slot, start_block):
    particles, radial_rows, angles = polar_images.shape
    rank, width = start_block.shape[1:]
    slots = order_of_slot.shape[0]
    blocks = (NPLANE, NZ, 2 * particles, radial_rows)
    vmem = pl.BlockSpec(memory_space=pltpu.VMEM)
    smem = pl.BlockSpec(memory_space=pltpu.SMEM)
    anywhere = pl.BlockSpec(memory_space=pl.ANY)
    table, mine = pl.pallas_call(
        whole_kernel,
        out_shape=(
            jax.ShapeDtypeStruct((2 * slots, angles), jnp.bfloat16),
            jax.ShapeDtypeStruct(blocks, jnp.bfloat16),
        ),
        in_specs=[vmem, anywhere, smem, smem, vmem, anywhere],
        out_specs=(vmem, vmem),
        scratch_shapes=[
            pltpu.VMEM((slots * 2 * particles, radial_rows), jnp.float32),
            pltpu.VMEM(blocks, jnp.bfloat16),
            pltpu.VMEM(blocks, jnp.bfloat16),
            pltpu.VMEM((NZ, radial_rows, width), jnp.bfloat16),
            pltpu.VMEM((NZ, NPLANE * 2 * particles, width), jnp.bfloat16),
            pltpu.VMEM((width, width), jnp.float32),
            pltpu.VMEM((NZ, width, width), jnp.bfloat16),
            pltpu.VMEM((NZ, width, width), jnp.bfloat16),
            pltpu.VMEM((rank, width), jnp.bfloat16),
            pltpu.VMEM((NZ, rank, width), jnp.bfloat16),
            pltpu.VMEM(blocks, jnp.bfloat16),
            pltpu.VMEM((rank, width), jnp.float32),
            *[pltpu.SemaphoreType.DMA] * 12,
        ],
        compiler_params=pltpu.CompilerParams(collective_id=0, has_side_effects=True),
        name="whole",
    )(
        polar_images,
        radial_basis,
        radial_start,
        radial_count,
        order_of_slot.reshape(2, slots // 2),
        start_block,
    )
    mine = mine.reshape(slots, 2, particles, radial_rows)
    table = table.reshape(2, slots, angles)
    denoised = jnp.einsum("scpr,cst->prt", mine, table, preferred_element_type=jnp.float32)
    return denoised.astype(jnp.bfloat16)


def solution(mesh):
    placed = (
        P(("dom", "ord"), None, None),
        P("ord", None, None),
        P("ord"),
        P("ord"),
        P(),
        P("ord", None, None),
    )
    return jax.shard_map(
        on_device,
        mesh=mesh,
        in_specs=placed,
        out_specs=P(("dom", "ord"), None, None),
        check_vma=False,
    )
```

```python
import math

import jax
import jax.numpy as jnp
from jax import lax
from jax.experimental import pallas as pl
from jax.experimental.pallas import tpu as pltpu
from jax.sharding import PartitionSpec as P

NRB = 8
ITERS = 4
NZ, NY, NX = 8, 4, 4
NDOM = NZ * NY * NX
NPLANE = 2 * NY * NX
MESH = pl.DeviceIdType.MESH


FAR_FIRST_8 = (4, 3, 5, 2, 6, 1, 7, 0)
FAR_FIRST_4 = (2, 1, 3, 0)
SLOT_PARTS = ((0, 1, 2, 3), (4, 5, 6, 7))


def dot32(a, b, dims):
    return lax.dot_general(
        a, b, (dims, ((), ())), precision=lax.Precision.HIGHEST, preferred_element_type=jnp.float32
    )


def orthonormal(image_t):
    rank, width = image_t.shape
    gram = dot32(image_t, image_t, ((1,), (1,)))
    lane_block = lax.broadcasted_iota(jnp.int32, (rank, rank * width), 1) // width
    spread = lane_block == lax.broadcasted_iota(jnp.int32, (rank, rank * width), 0)
    wide = dot32(gram, spread.astype(jnp.float32), ((1,), (0,)))
    cols = [wide[:, j * width : (j + 1) * width] for j in range(rank)]
    row_id = lax.broadcasted_iota(jnp.int32, (rank, width), 0)
    pivots = jnp.ones((rank, width), jnp.float32)
    out = image_t
    for j in range(rank):
        pivot = jnp.broadcast_to(cols[j][j : j + 1, :], (rank, width))
        pivots = jnp.where(row_id == j, pivot, pivots)
        factor = jnp.where(row_id > j, cols[j] / pivot, 0.0)
        for k in range(j + 1, rank):
            cols[k] = cols[k] - factor * cols[k][j : j + 1, :]
        out = out - factor * out[j : j + 1, :]
    return out / jnp.sqrt(pivots)


def place():
    d = lax.axis_index("dom")
    return d, lax.axis_index("ord"), d // (NY * NX), (d // NX) % NY, d % NX


def z_peers():
    d, o, z, y, x = place()
    for k in FAR_FIRST_8[:-1]:
        pz = (z + k) % NZ
        yield pz, pz * (NY * NX) + y * NX + x


def plane_peers():
    d, o, z, y, x = place()
    at_y = [(y + k) % NY * NX for k in range(NY)]
    at_x = [(x + k) % NX for k in range(NX)]
    for dy in FAR_FIRST_4:
        for dx in FAR_FIRST_4:
            m = at_y[dy] + at_x[dx]
            for po in (1 - o, o) if (dy, dx) != (0, 0) else (1 - o,):
                yield po * (NY * NX) + m, z * (NY * NX) + m, po


def remote(src_ref, dst_ref, send_sem, recv_sem, device):
    return pltpu.make_async_remote_copy(
        src_ref=src_ref,
        dst_ref=dst_ref,
        send_sem=send_sem,
        recv_sem=recv_sem,
        device_id=device,
        device_id_type=MESH,
    )


def wait_blocks(src_ref, dst_ref, send_sem, recv_sem, blocks):
    d, o = place()[:2]
    most = pl.ds(0, blocks)
    everything = remote(src_ref.at[most], dst_ref.at[most], send_sem, recv_sem, (d, 1 - o))
    everything.wait_send()
    everything.wait_recv()


def plane_exchange(src_ref, dst_ref, send_sem, recv_sem, own_sem):
    d, o, z, y, x = place()
    mine = o * (NY * NX) + y * NX + x
    for index, pd, po in plane_peers():
        remote(src_ref.at[index], dst_ref.at[mine], send_sem, recv_sem, (pd, po)).start()
    own = pltpu.make_async_copy(src_ref.at[mine], dst_ref.at[mine], own_sem)
    own.start()
    own.wait()
    wait_blocks(src_ref, dst_ref, send_sem, recv_sem, NPLANE - 1)


def fill_table(order_ref, table_ref):
    angles = table_ref.shape[1]
    weight = math.sqrt(2.0 / angles)
    for half in range(2):
        row = order_ref[half : half + 1, :].astype(jnp.float32)
        k = jnp.broadcast_to(row, (128, 128)).T.astype(jnp.int32)
        lane = lax.broadcasted_iota(jnp.int32, (128, 128), 1)
        turn = (k * lane) & (angles - 1)
        quarter = (turn + angles // 8) >> 7
        angle = (turn - quarter * (angles // 4)).astype(jnp.float32) * (2.0 * math.pi / angles)
        sq = angle * angle
        cos = 1.0 + sq * (-1 / 2 + sq * (1 / 24 + sq * (-1 / 720 + sq * (1 / 40320))))
        sin = angle * (1.0 + sq * (-1 / 6 + sq * (1 / 120 + sq * (-1 / 5040 + sq * (1 / 362880)))))
        cos = cos * weight
        sin = sin * weight
        for b in range(angles // 128):
            quadrant = (quarter + b * k) & 3
            odd = (quadrant & 1) == 1
            upper = quadrant >= 2
            even_sign = jnp.where(upper, -1.0, 1.0)
            real = jnp.where(odd, -sin, cos) * even_sign
            imag = jnp.where(odd, -cos, -sin) * even_sign
            span = slice(128 * b, 128 * (b + 1))
            table_ref[128 * half : 128 * (half + 1), span] = real.astype(jnp.bfloat16)
            table_ref[256 + 128 * half : 256 + 128 * (half + 1), span] = imag.astype(jnp.bfloat16)


def fill_spectrum(table_ref, images_ref, wide_ref):
    slots = table_ref.shape[0] // 2
    for p in range(0, images_ref.shape[0], 2):
        pair = images_ref[p : p + 2].reshape(2 * images_ref.shape[1], images_ref.shape[2])
        for c in range(2):
            part = lax.dot_general(
                table_ref[slots * c : slots * (c + 1), :],
                pair,
                (((1,), (1,)), ((), ())),
                preferred_element_type=jnp.float32,
            )
            wide_ref[pl.ds(4 * c + p, slots, stride=8), :] = part[:, :128]
            wide_ref[pl.ds(4 * c + p + 1, slots, stride=8), :] = part[:, 128:]


def whole_kernel(
    images_ref,
    radial_ref,
    first_ref,
    count_ref,
    order_ref,
    start_ref,
    table_ref,
    out_ref,
    wide_ref,
    spec_ref,
    rows_ref,
    masked_ref,
    coef_ref,
    part_ref,
    given_ref,
    taken_ref,
    eig_ref,
    eigs_ref,
    prof_ref,
    start_own,
    send_1,
    recv_1,
    own_1,
    send_2,
    recv_2,
    send_3,
    recv_3,
    send_4,
    recv_4,
    own_4,
    load_1,
    load_2,
):
    d, o, z, y, x = place()
    first_slot = (y * NX + x) * NZ
    barrier = pltpu.get_barrier_semaphore()
    for _, pd in z_peers():
        pl.semaphore_signal(barrier, inc=1, device_id=(pd, o), device_id_type=MESH)
    for _, pd, po in plane_peers():
        pl.semaphore_signal(barrier, inc=1, device_id=(pd, po), device_id_type=MESH)
    radial_load = pltpu.make_async_copy(radial_ref.at[pl.ds(first_slot, NZ)], masked_ref, load_1)
    start_load = pltpu.make_async_copy(start_ref.at[first_slot + z], start_own, load_2)
    radial_load.start()
    start_load.start()
    fill_table(order_ref, table_ref)
    fill_spectrum(table_ref, images_ref, wide_ref)
    by_slot = wide_ref.reshape(NPLANE, NZ * 8, wide_ref.shape[1])
    for i, k in enumerate(FAR_FIRST_8):
        j = (z + k) % NZ
        slot_rows = by_slot[:, pl.ds(pl.multiple_of(j * 8, 8), 8), :]
        spec_ref[:, i] = slot_rows.astype(jnp.bfloat16)
    radial_load.wait()
    start_load.wait()
    radial_rows, width = masked_ref.shape[1:]
    row_id = lax.broadcasted_iota(jnp.int32, (radial_rows, width), 0)
    col_id = lax.broadcasted_iota(jnp.int32, (radial_rows, width), 1)
    for j in range(NZ):
        first_row = first_ref[first_slot + j] * (radial_rows // NRB)
        keep = (row_id >= first_row) & (col_id < count_ref[first_slot + j])
        masked = jnp.where(keep, masked_ref[j].astype(jnp.float32), 0.0)
        masked_ref[j] = masked.astype(jnp.bfloat16)
    pl.semaphore_wait(barrier, NPLANE - 1 + NZ - 1)
    mine = o * (NY * NX) + y * NX + x
    own = pltpu.make_async_copy(spec_ref.at[mine], rows_ref.at[mine], own_1)
    own.start()
    for part_id, slots in enumerate(SLOT_PARTS):
        span = pl.ds(slots[0], len(slots))
        for index, pd, po in plane_peers():
            remote(
                spec_ref.at[index, span],
                rows_ref.at[mine, span],
                send_1.at[part_id],
                recv_1.at[part_id],
                (pd, po),
            ).start()
    own.wait()

    waiting = None
    for i, (j, pd) in enumerate([*z_peers(), (z, None)]):
        for part_id, slots in enumerate(SLOT_PARTS):
            if i == slots[0]:
                span = pl.ds(slots[0], len(slots))
                wait_blocks(
                    spec_ref.at[:, span],
                    rows_ref.at[:, span],
                    send_1.at[part_id],
                    recv_1.at[part_id],
                    NPLANE - 1,
                )
        rows = rows_ref[:, i].astype(jnp.float32).reshape(NPLANE * 8, radial_rows).astype(jnp.bfloat16)
        coef = jnp.dot(rows, masked_ref[j], preferred_element_type=jnp.float32).astype(jnp.bfloat16)
        coef_ref[j] = coef
        part = lax.dot_general(
            coef, coef, (((0,), (0,)), ((), ())), preferred_element_type=jnp.float32
        )
        if pd is not None:
            given_ref[j] = part.astype(jnp.bfloat16)
        if waiting is not None:
            waiting.start()
        if pd is not None:
            waiting = remote(given_ref.at[j], taken_ref.at[z], send_2, recv_2, (pd, o))
    part_ref[...] = part
    wait_blocks(given_ref, taken_ref, send_2, recv_2, NZ - 1)
    cov = part_ref[...]
    for k in range(1, NZ):
        cov = cov + taken_ref[(z + k) % NZ].astype(jnp.float32)

    basis_t = start_own[...]
    for step in range(ITERS):
        basis_t = orthonormal(dot32(basis_t, cov, ((1,), (0,))))
    eig_t = basis_t.astype(jnp.bfloat16)
    eig_ref[...] = eig_t
    eigs_ref[z] = eig_t
    for _, pd in z_peers():
        remote(eig_ref, eigs_ref.at[z], send_3, recv_3, (pd, o)).start()
    wait_blocks(eigs_ref, eigs_ref, send_3, recv_3, NZ - 1)

    for j in range(NZ):
        eig_t = eigs_ref[j]
        u_t = lax.dot_general(
            eig_t, masked_ref[j], (((1,), (1,)), ((), ())), preferred_element_type=jnp.float32
        ).astype(jnp.bfloat16)
        scores = lax.dot_general(
            coef_ref[j], eig_t, (((1,), (1,)), ((), ())), preferred_element_type=jnp.float32
        ).astype(jnp.bfloat16)
        profile = jnp.dot(scores, u_t, preferred_element_type=jnp.float32)
        prof_ref[:, j] = profile.reshape(NPLANE, 8, radial_rows).astype(jnp.bfloat16)
    plane_exchange(prof_ref, out_ref, send_4, recv_4, own_4)


def on_device(polar_images, radial_basis, radial_start, radial_count, order_of_slot, start_block):
    particles, radial_rows, angles = polar_images.shape
    rank, width = start_block.shape[1:]
    slots = order_of_slot.shape[0]
    blocks = (NPLANE, NZ, 2 * particles, radial_rows)
    vmem = pl.BlockSpec(memory_space=pltpu.VMEM)
    smem = pl.BlockSpec(memory_space=pltpu.SMEM)
    anywhere = pl.BlockSpec(memory_space=pl.ANY)
    table, mine = pl.pallas_call(
        whole_kernel,
        out_shape=(
            jax.ShapeDtypeStruct((2 * slots, angles), jnp.bfloat16),
            jax.ShapeDtypeStruct(blocks, jnp.bfloat16),
        ),
        in_specs=[vmem, anywhere, smem, smem, vmem, anywhere],
        out_specs=(vmem, vmem),
        scratch_shapes=[
            pltpu.VMEM((slots * 2 * particles, radial_rows), jnp.float32),
            pltpu.VMEM(blocks, jnp.bfloat16),
            pltpu.VMEM(blocks, jnp.bfloat16),
            pltpu.VMEM((NZ, radial_rows, width), jnp.bfloat16),
            pltpu.VMEM((NZ, NPLANE * 2 * particles, width), jnp.bfloat16),
            pltpu.VMEM((width, width), jnp.float32),
            pltpu.VMEM((NZ, width, width), jnp.bfloat16),
            pltpu.VMEM((NZ, width, width), jnp.bfloat16),
            pltpu.VMEM((rank, width), jnp.bfloat16),
            pltpu.VMEM((NZ, rank, width), jnp.bfloat16),
            pltpu.VMEM(blocks, jnp.bfloat16),
            pltpu.VMEM((rank, width), jnp.float32),
            *[pltpu.SemaphoreType.DMA((len(SLOT_PARTS),))] * 2,
            *[pltpu.SemaphoreType.DMA] * 10,
        ],
        compiler_params=pltpu.CompilerParams(collective_id=0, has_side_effects=True),
        name="whole",
    )(
        polar_images,
        radial_basis,
        radial_start,
        radial_count,
        order_of_slot.reshape(2, slots // 2),
        start_block,
    )
    mine = mine.reshape(slots, 2, particles, radial_rows)
    table = table.reshape(2, slots, angles)
    denoised = jnp.einsum("scpr,cst->prt", mine, table, preferred_element_type=jnp.float32)
    return denoised.astype(jnp.bfloat16)


def solution(mesh):
    placed = (
        P(("dom", "ord"), None, None),
        P("ord", None, None),
        P("ord"),
        P("ord"),
        P(),
        P("ord", None, None),
    )
    return jax.shard_map(
        on_device,
        mesh=mesh,
        in_specs=placed,
        out_specs=P(("dom", "ord"), None, None),
        check_vma=False,
    )
```

```python
import math

import jax
import jax.numpy as jnp
from jax import lax
from jax.experimental import pallas as pl
from jax.experimental.pallas import tpu as pltpu
from jax.sharding import PartitionSpec as P

NRB = 8
ITERS = 4
NZ, NY, NX = 8, 4, 4
NDOM = NZ * NY * NX
NPLANE = 2 * NY * NX
MESH = pl.DeviceIdType.MESH


FAR_FIRST_8 = (4, 3, 5, 2, 6, 1, 7, 0)
FAR_FIRST_4 = (2, 1, 3, 0)
SLOT_PARTS = ((0, 1), (2, 3), (4, 5), (6, 7))


def dot32(a, b, dims):
    return lax.dot_general(
        a, b, (dims, ((), ())), precision=lax.Precision.HIGHEST, preferred_element_type=jnp.float32
    )


def orthonormal(image_t):
    rank, width = image_t.shape
    gram = dot32(image_t, image_t, ((1,), (1,)))
    lane_block = lax.broadcasted_iota(jnp.int32, (rank, rank * width), 1) // width
    spread = lane_block == lax.broadcasted_iota(jnp.int32, (rank, rank * width), 0)
    wide = dot32(gram, spread.astype(jnp.float32), ((1,), (0,)))
    cols = [wide[:, j * width : (j + 1) * width] for j in range(rank)]
    row_id = lax.broadcasted_iota(jnp.int32, (rank, width), 0)
    pivots = jnp.ones((rank, width), jnp.float32)
    out = image_t
    for j in range(rank):
        pivot = jnp.broadcast_to(cols[j][j : j + 1, :], (rank, width))
        pivots = jnp.where(row_id == j, pivot, pivots)
        factor = jnp.where(row_id > j, cols[j] / pivot, 0.0)
        for k in range(j + 1, rank):
            cols[k] = cols[k] - factor * cols[k][j : j + 1, :]
        out = out - factor * out[j : j + 1, :]
    return out / jnp.sqrt(pivots)


def place():
    d = lax.axis_index("dom")
    return d, lax.axis_index("ord"), d // (NY * NX), (d // NX) % NY, d % NX


def z_peers():
    d, o, z, y, x = place()
    for i, k in enumerate(FAR_FIRST_8[:-1]):
        pd = (z + k) % NZ * (NY * NX) + y * NX + x
        yield i, FAR_FIRST_8.index((NZ - k) % NZ), pd


def plane_peers():
    d, o, z, y, x = place()
    at_y = [(y + k) % NY * NX for k in range(NY)]
    at_x = [(x + k) % NX for k in range(NX)]
    for dy in FAR_FIRST_4:
        for dx in FAR_FIRST_4:
            m = at_y[dy] + at_x[dx]
            for po in (1 - o, o) if (dy, dx) != (0, 0) else (1 - o,):
                yield po * (NY * NX) + m, z * (NY * NX) + m, po


def remote(src_ref, dst_ref, send_sem, recv_sem, device):
    return pltpu.make_async_remote_copy(
        src_ref=src_ref,
        dst_ref=dst_ref,
        send_sem=send_sem,
        recv_sem=recv_sem,
        device_id=device,
        device_id_type=MESH,
    )


def wait_blocks(src_ref, dst_ref, send_sem, recv_sem, blocks):
    d, o = place()[:2]
    most = pl.ds(0, blocks)
    everything = remote(src_ref.at[most], dst_ref.at[most], send_sem, recv_sem, (d, 1 - o))
    everything.wait_send()
    everything.wait_recv()


def own_block(src_ref, dst_ref, own_sem):
    d, o, z, y, x = place()
    mine = o * (NY * NX) + y * NX + x
    return pltpu.make_async_copy(src_ref.at[mine], dst_ref.at[mine], own_sem)


def send_part(part, src_ref, dst_ref, send_sem, recv_sem):
    d, o, z, y, x = place()
    mine = o * (NY * NX) + y * NX + x
    span = pl.ds(SLOT_PARTS[part][0], len(SLOT_PARTS[part]))
    for index, pd, po in plane_peers():
        remote(
            src_ref.at[index, span],
            dst_ref.at[mine, span],
            send_sem.at[part],
            recv_sem.at[part],
            (pd, po),
        ).start()


def wait_part(part, src_ref, dst_ref, send_sem, recv_sem):
    span = pl.ds(SLOT_PARTS[part][0], len(SLOT_PARTS[part]))
    wait_blocks(
        src_ref.at[:, span], dst_ref.at[:, span], send_sem.at[part], recv_sem.at[part], NPLANE - 1
    )


def fill_table(order_ref, table_ref):
    angles = table_ref.shape[1]
    weight = math.sqrt(2.0 / angles)
    z = place()[2]
    row_id = lax.broadcasted_iota(jnp.int32, (128, 128), 0)
    lane = lax.broadcasted_iota(jnp.int32, (128, 128), 1)
    spot = row_id & (NZ - 1)
    step = (spot + 1) >> 1
    offset = NZ // 2 + jnp.where((spot & 1) == 1, -step, step)
    chosen = lane == row_id - spot + ((z + offset) & (NZ - 1))
    chosen = jnp.where(chosen, 1.0, 0.0).astype(jnp.bfloat16)
    for half in range(2):
        row = order_ref[half : half + 1, :].astype(jnp.float32)
        k = lax.dot_general(
            chosen,
            jnp.broadcast_to(row, (128, 128)).astype(jnp.bfloat16),
            (((1,), (1,)), ((), ())),
            preferred_element_type=jnp.float32,
        ).astype(jnp.int32)
        turn = (k * lane) & (angles - 1)
        quarter = (turn + angles // 8) >> 7
        angle = (turn - quarter * (angles // 4)).astype(jnp.float32) * (2.0 * math.pi / angles)
        sq = angle * angle
        cos = 1.0 + sq * (-1 / 2 + sq * (1 / 24 + sq * (-1 / 720 + sq * (1 / 40320))))
        sin = angle * (1.0 + sq * (-1 / 6 + sq * (1 / 120 + sq * (-1 / 5040 + sq * (1 / 362880)))))
        cos = cos * weight
        sin = sin * weight
        for b in range(angles // 128):
            quadrant = (quarter + b * k) & 3
            odd = (quadrant & 1) == 1
            upper = quadrant >= 2
            even_sign = jnp.where(upper, -1.0, 1.0)
            real = jnp.where(odd, -sin, cos) * even_sign
            imag = jnp.where(odd, -cos, -sin) * even_sign
            span = slice(128 * b, 128 * (b + 1))
            table_ref[128 * half : 128 * (half + 1), span] = real.astype(jnp.bfloat16)
            table_ref[256 + 128 * half : 256 + 128 * (half + 1), span] = imag.astype(jnp.bfloat16)


def fill_spectrum(table_ref, images_ref, wide_ref):
    slots = table_ref.shape[0] // 2
    for p in range(0, images_ref.shape[0], 2):
        pair = images_ref[p : p + 2].reshape(2 * images_ref.shape[1], images_ref.shape[2])
        for c in range(2):
            part = lax.dot_general(
                table_ref[slots * c : slots * (c + 1), :],
                pair,
                (((1,), (1,)), ((), ())),
                preferred_element_type=jnp.float32,
            )
            wide_ref[pl.ds(4 * c + p, slots, stride=8), :] = part[:, :128]
            wide_ref[pl.ds(4 * c + p + 1, slots, stride=8), :] = part[:, 128:]


def whole_kernel(
    images_ref,
    radial_ref,
    first_ref,
    count_ref,
    order_ref,
    start_ref,
    table_ref,
    out_ref,
    wide_ref,
    spec_ref,
    rows_ref,
    radial_own,
    masked_ref,
    coef_ref,
    part_ref,
    given_ref,
    taken_ref,
    eigs_ref,
    prof_ref,
    start_own,
    send_1,
    recv_1,
    send_4,
    recv_4,
    send_3,
    recv_3,
    send_2,
    recv_2,
    own_1,
    own_4,
    load_1,
    load_2,
):
    d, o, z, y, x = place()
    first_slot = (y * NX + x) * NZ
    barrier = pltpu.get_barrier_semaphore()
    for _, _, pd in z_peers():
        pl.semaphore_signal(barrier, inc=1, device_id=(pd, o), device_id_type=MESH)
    for _, pd, po in plane_peers():
        pl.semaphore_signal(barrier, inc=1, device_id=(pd, po), device_id_type=MESH)
    radial_load = pltpu.make_async_copy(radial_ref.at[pl.ds(first_slot, NZ)], radial_own, load_1)
    start_load = pltpu.make_async_copy(start_ref.at[first_slot + z], start_own, load_2)
    radial_load.start()
    start_load.start()
    fill_table(order_ref, table_ref)
    fill_spectrum(table_ref, images_ref, wide_ref)
    spec_ref[...] = wide_ref[...].reshape(spec_ref.shape).astype(jnp.bfloat16)
    radial_load.wait()
    start_load.wait()
    radial_rows, width = masked_ref.shape[1:]
    row_id = lax.broadcasted_iota(jnp.int32, (radial_rows, width), 0)
    col_id = lax.broadcasted_iota(jnp.int32, (radial_rows, width), 1)
    for i, k in enumerate(FAR_FIRST_8):
        j = (z + k) % NZ
        first_row = first_ref[first_slot + j] * (radial_rows // NRB)
        keep = (row_id >= first_row) & (col_id < count_ref[first_slot + j])
        masked = jnp.where(keep, radial_own[j].astype(jnp.float32), 0.0)
        masked_ref[i] = masked.astype(jnp.bfloat16)
    pl.semaphore_wait(barrier, NPLANE - 1 + NZ - 1)
    own = own_block(spec_ref, rows_ref, own_1)
    own.start()
    for part in range(len(SLOT_PARTS)):
        send_part(part, spec_ref, rows_ref, send_1, recv_1)
    own.wait()

    peers = list(z_peers())
    waiting = None
    for part, spots in enumerate(SLOT_PARTS):
        wait_part(part, spec_ref, rows_ref, send_1, recv_1)
        for i in spots:
            rows = rows_ref[:, i].astype(jnp.float32).reshape(NPLANE * 8, radial_rows)
            coef = jnp.dot(
                rows.astype(jnp.bfloat16), masked_ref[i], preferred_element_type=jnp.float32
            ).astype(jnp.bfloat16)
            coef_ref[i] = coef
            cov = lax.dot_general(
                coef, coef, (((0,), (0,)), ((), ())), preferred_element_type=jnp.float32
            )
            if i < len(peers):
                given_ref[i] = cov.astype(jnp.bfloat16)
            else:
                part_ref[...] = cov
            if waiting is not None:
                waiting.start()
            if i < len(peers):
                _, there, pd = peers[i]
                waiting = remote(given_ref.at[i], taken_ref.at[there], send_2, recv_2, (pd, o))
    wait_blocks(given_ref, taken_ref, send_2, recv_2, NZ - 1)
    cov = part_ref[...]
    for i in range(NZ - 1):
        cov = cov + taken_ref[i].astype(jnp.float32)

    basis_t = start_own[...]
    for step in range(ITERS):
        basis_t = orthonormal(dot32(basis_t, cov, ((1,), (0,))))
    eig_t = basis_t.astype(jnp.bfloat16)
    eigs_ref[NZ - 1] = eig_t
    for i, there, pd in peers:
        remote(
            eigs_ref.at[NZ - 1], eigs_ref.at[there], send_3.at[i], recv_3.at[there], (pd, o)
        ).start()

    for part in reversed(range(len(SLOT_PARTS))):
        for i in reversed(SLOT_PARTS[part]):
            if i < len(peers):
                remote(
                    eigs_ref.at[i], eigs_ref.at[i], send_3.at[i], recv_3.at[i], (peers[i][2], o)
                ).wait_recv()
            eig_t = eigs_ref[i]
            u_t = lax.dot_general(
                eig_t, masked_ref[i], (((1,), (1,)), ((), ())), preferred_element_type=jnp.float32
            ).astype(jnp.bfloat16)
            scores = lax.dot_general(
                coef_ref[i], eig_t, (((1,), (1,)), ((), ())), preferred_element_type=jnp.float32
            ).astype(jnp.bfloat16)
            profile = jnp.dot(scores, u_t, preferred_element_type=jnp.float32)
            prof_ref[:, i] = profile.reshape(NPLANE, 8, radial_rows).astype(jnp.bfloat16)
        send_part(part, prof_ref, out_ref, send_4, recv_4)
    own = own_block(prof_ref, out_ref, own_4)
    own.start()
    for i, _, pd in peers:
        remote(
            eigs_ref.at[NZ - 1], eigs_ref.at[i], send_3.at[i], recv_3.at[i], (pd, o)
        ).wait_send()
    own.wait()
    for part in reversed(range(len(SLOT_PARTS))):
        wait_part(part, prof_ref, out_ref, send_4, recv_4)


def on_device(polar_images, radial_basis, radial_start, radial_count, order_of_slot, start_block):
    particles, radial_rows, angles = polar_images.shape
    rank, width = start_block.shape[1:]
    slots = order_of_slot.shape[0]
    blocks = (NPLANE, NZ, 2 * particles, radial_rows)
    vmem = pl.BlockSpec(memory_space=pltpu.VMEM)
    smem = pl.BlockSpec(memory_space=pltpu.SMEM)
    anywhere = pl.BlockSpec(memory_space=pl.ANY)
    table, mine = pl.pallas_call(
        whole_kernel,
        out_shape=(
            jax.ShapeDtypeStruct((2 * slots, angles), jnp.bfloat16),
            jax.ShapeDtypeStruct(blocks, jnp.bfloat16),
        ),
        in_specs=[vmem, anywhere, smem, smem, vmem, anywhere],
        out_specs=(vmem, vmem),
        scratch_shapes=[
            pltpu.VMEM((slots * 2 * particles, radial_rows), jnp.float32),
            pltpu.VMEM(blocks, jnp.bfloat16),
            pltpu.VMEM(blocks, jnp.bfloat16),
            pltpu.VMEM((NZ, radial_rows, width), jnp.bfloat16),
            pltpu.VMEM((NZ, radial_rows, width), jnp.bfloat16),
            pltpu.VMEM((NZ, NPLANE * 2 * particles, width), jnp.bfloat16),
            pltpu.VMEM((width, width), jnp.float32),
            pltpu.VMEM((NZ, width, width), jnp.bfloat16),
            pltpu.VMEM((NZ, width, width), jnp.bfloat16),
            pltpu.VMEM((NZ, rank, width), jnp.bfloat16),
            pltpu.VMEM(blocks, jnp.bfloat16),
            pltpu.VMEM((rank, width), jnp.float32),
            *[pltpu.SemaphoreType.DMA((len(SLOT_PARTS),))] * 4,
            *[pltpu.SemaphoreType.DMA((NZ - 1,))] * 2,
            *[pltpu.SemaphoreType.DMA] * 6,
        ],
        compiler_params=pltpu.CompilerParams(collective_id=0, has_side_effects=True),
        name="whole",
    )(
        polar_images,
        radial_basis,
        radial_start,
        radial_count,
        order_of_slot.reshape(2, slots // 2),
        start_block,
    )
    mine = mine.reshape(slots, 2, particles, radial_rows)
    table = table.reshape(2, slots, angles)
    denoised = jnp.einsum("scpr,cst->prt", mine, table, preferred_element_type=jnp.float32)
    return denoised.astype(jnp.bfloat16)


def solution(mesh):
    placed = (
        P(("dom", "ord"), None, None),
        P("ord", None, None),
        P("ord"),
        P("ord"),
        P(),
        P("ord", None, None),
    )
    return jax.shard_map(
        on_device,
        mesh=mesh,
        in_specs=placed,
        out_specs=P(("dom", "ord"), None, None),
        check_vma=False,
    )
```

```python
import math

import jax
import jax.numpy as jnp
from jax import lax
from jax.experimental import pallas as pl
from jax.experimental.pallas import tpu as pltpu
from jax.sharding import PartitionSpec as P

NRB = 8
ITERS = 4
NZ, NY, NX = 8, 4, 4
NDOM = NZ * NY * NX
NPLANE = 2 * NY * NX
MESH = pl.DeviceIdType.MESH


FAR_FIRST_8 = (4, 3, 5, 2, 6, 1, 7, 0)
FAR_FIRST_4 = (2, 1, 3, 0)
SLOT_PARTS = ((0, 1), (2, 3), (4, 5), (6, 7))


def dot32(a, b, dims):
    return lax.dot_general(
        a, b, (dims, ((), ())), precision=lax.Precision.HIGHEST, preferred_element_type=jnp.float32
    )


def split(value, pieces):
    out = []
    for _ in range(pieces):
        piece = value.astype(jnp.bfloat16)
        value = value - piece.astype(jnp.float32)
        out.append(piece)
    return out


def times_cov(basis_t, cov_high, cov_low):
    rank = basis_t.shape[0]
    high, low = split(basis_t, 2)
    both = jnp.dot(
        jnp.concatenate([high, low], axis=0), cov_high, preferred_element_type=jnp.float32
    )
    rest = jnp.dot(high, cov_low, preferred_element_type=jnp.float32)
    return both[:rank] + (both[rank:] + rest)


def orthonormal(image_t):
    rank, width = image_t.shape
    gram = dot32(image_t, image_t, ((1,), (1,)))
    lane_block = lax.broadcasted_iota(jnp.int32, (rank, rank * width), 1) // width
    spread = lane_block == lax.broadcasted_iota(jnp.int32, (rank, rank * width), 0)
    pieces = jnp.concatenate(split(gram, 3), axis=0)
    wide = jnp.dot(
        pieces, jnp.where(spread, 1.0, 0.0).astype(jnp.bfloat16), preferred_element_type=jnp.float32
    )
    wide = wide[:rank] + wide[rank : 2 * rank] + wide[2 * rank :]
    cols = [wide[:, j * width : (j + 1) * width] for j in range(rank)]
    row_id = lax.broadcasted_iota(jnp.int32, (rank, width), 0)
    pivots = jnp.ones((rank, width), jnp.float32)
    out = image_t
    for j in range(rank):
        pivot = jnp.broadcast_to(cols[j][j : j + 1, :], (rank, width))
        pivots = jnp.where(row_id == j, pivot, pivots)
        factor = jnp.where(row_id > j, cols[j] / pivot, 0.0)
        for k in range(j + 1, rank):
            cols[k] = cols[k] - factor * cols[k][j : j + 1, :]
        out = out - factor * out[j : j + 1, :]
    return out / jnp.sqrt(pivots)


def place():
    d = lax.axis_index("dom")
    return d, lax.axis_index("ord"), d // (NY * NX), (d // NX) % NY, d % NX


def z_peers():
    d, o, z, y, x = place()
    for i, k in enumerate(FAR_FIRST_8[:-1]):
        pd = (z + k) % NZ * (NY * NX) + y * NX + x
        yield i, FAR_FIRST_8.index((NZ - k) % NZ), pd


def plane_peers():
    d, o, z, y, x = place()
    at_y = [(y + k) % NY * NX for k in range(NY)]
    at_x = [(x + k) % NX for k in range(NX)]
    for dy in FAR_FIRST_4:
        for dx in FAR_FIRST_4:
            m = at_y[dy] + at_x[dx]
            for po in (1 - o, o) if (dy, dx) != (0, 0) else (1 - o,):
                yield po * (NY * NX) + m, z * (NY * NX) + m, po


def remote(src_ref, dst_ref, send_sem, recv_sem, device):
    return pltpu.make_async_remote_copy(
        src_ref=src_ref,
        dst_ref=dst_ref,
        send_sem=send_sem,
        recv_sem=recv_sem,
        device_id=device,
        device_id_type=MESH,
    )


def wait_blocks(src_ref, dst_ref, send_sem, recv_sem, blocks):
    d, o = place()[:2]
    most = pl.ds(0, blocks)
    everything = remote(src_ref.at[most], dst_ref.at[most], send_sem, recv_sem, (d, 1 - o))
    everything.wait_send()
    everything.wait_recv()


def own_block(src_ref, dst_ref, own_sem):
    d, o, z, y, x = place()
    mine = o * (NY * NX) + y * NX + x
    return pltpu.make_async_copy(src_ref.at[mine], dst_ref.at[mine], own_sem)


def send_part(part, src_ref, dst_ref, send_sem, recv_sem):
    d, o, z, y, x = place()
    mine = o * (NY * NX) + y * NX + x
    span = pl.ds(SLOT_PARTS[part][0], len(SLOT_PARTS[part]))
    for index, pd, po in plane_peers():
        remote(
            src_ref.at[index, span],
            dst_ref.at[mine, span],
            send_sem.at[part],
            recv_sem.at[part],
            (pd, po),
        ).start()


def wait_part(part, src_ref, dst_ref, send_sem, recv_sem):
    span = pl.ds(SLOT_PARTS[part][0], len(SLOT_PARTS[part]))
    wait_blocks(
        src_ref.at[:, span], dst_ref.at[:, span], send_sem.at[part], recv_sem.at[part], NPLANE - 1
    )


def fill_table(order_ref, table_ref):
    angles = table_ref.shape[1]
    weight = math.sqrt(2.0 / angles)
    z = place()[2]
    row_id = lax.broadcasted_iota(jnp.int32, (128, 128), 0)
    lane = lax.broadcasted_iota(jnp.int32, (128, 128), 1)
    spot = row_id & (NZ - 1)
    step = (spot + 1) >> 1
    offset = NZ // 2 + jnp.where((spot & 1) == 1, -step, step)
    chosen = lane == row_id - spot + ((z + offset) & (NZ - 1))
    chosen = jnp.where(chosen, 1.0, 0.0).astype(jnp.bfloat16)
    for half in range(2):
        row = order_ref[half : half + 1, :].astype(jnp.float32)
        k = lax.dot_general(
            chosen,
            jnp.broadcast_to(row, (128, 128)).astype(jnp.bfloat16),
            (((1,), (1,)), ((), ())),
            preferred_element_type=jnp.float32,
        ).astype(jnp.int32)
        turn = (k * lane) & (angles - 1)
        quarter = (turn + angles // 8) >> 7
        angle = (turn - quarter * (angles // 4)).astype(jnp.float32) * (2.0 * math.pi / angles)
        sq = angle * angle
        cos = 1.0 + sq * (-1 / 2 + sq * (1 / 24 + sq * (-1 / 720 + sq * (1 / 40320))))
        sin = angle * (1.0 + sq * (-1 / 6 + sq * (1 / 120 + sq * (-1 / 5040 + sq * (1 / 362880)))))
        cos = cos * weight
        sin = sin * weight
        for b in range(angles // 128):
            quadrant = (quarter + b * k) & 3
            odd = (quadrant & 1) == 1
            upper = quadrant >= 2
            even_sign = jnp.where(upper, -1.0, 1.0)
            real = jnp.where(odd, -sin, cos) * even_sign
            imag = jnp.where(odd, -cos, -sin) * even_sign
            span = slice(128 * b, 128 * (b + 1))
            table_ref[128 * half : 128 * (half + 1), span] = real.astype(jnp.bfloat16)
            table_ref[256 + 128 * half : 256 + 128 * (half + 1), span] = imag.astype(jnp.bfloat16)


def fill_spectrum(table_ref, images_ref, wide_ref):
    slots = table_ref.shape[0] // 2
    for p in range(0, images_ref.shape[0], 2):
        pair = images_ref[p : p + 2].reshape(2 * images_ref.shape[1], images_ref.shape[2])
        for c in range(2):
            part = lax.dot_general(
                table_ref[slots * c : slots * (c + 1), :],
                pair,
                (((1,), (1,)), ((), ())),
                preferred_element_type=jnp.float32,
            )
            wide_ref[pl.ds(4 * c + p, slots, stride=8), :] = part[:, :128]
            wide_ref[pl.ds(4 * c + p + 1, slots, stride=8), :] = part[:, 128:]


def whole_kernel(
    images_ref,
    radial_ref,
    first_ref,
    count_ref,
    order_ref,
    start_ref,
    table_ref,
    out_ref,
    wide_ref,
    spec_ref,
    rows_ref,
    radial_own,
    masked_ref,
    coef_ref,
    part_ref,
    given_ref,
    taken_ref,
    eigs_ref,
    prof_ref,
    start_own,
    send_1,
    recv_1,
    send_4,
    recv_4,
    send_3,
    recv_3,
    send_2,
    recv_2,
    own_1,
    own_4,
    load_1,
    load_2,
):
    d, o, z, y, x = place()
    first_slot = (y * NX + x) * NZ
    barrier = pltpu.get_barrier_semaphore()
    for _, _, pd in z_peers():
        pl.semaphore_signal(barrier, inc=1, device_id=(pd, o), device_id_type=MESH)
    for _, pd, po in plane_peers():
        pl.semaphore_signal(barrier, inc=1, device_id=(pd, po), device_id_type=MESH)
    radial_load = pltpu.make_async_copy(radial_ref.at[pl.ds(first_slot, NZ)], radial_own, load_1)
    start_load = pltpu.make_async_copy(start_ref.at[first_slot + z], start_own, load_2)
    radial_load.start()
    start_load.start()
    fill_table(order_ref, table_ref)
    fill_spectrum(table_ref, images_ref, wide_ref)
    spec_ref[...] = wide_ref[...].reshape(spec_ref.shape).astype(jnp.bfloat16)
    radial_load.wait()
    start_load.wait()
    radial_rows, width = masked_ref.shape[1:]
    row_id = lax.broadcasted_iota(jnp.int32, (radial_rows, width), 0)
    col_id = lax.broadcasted_iota(jnp.int32, (radial_rows, width), 1)
    for i, k in enumerate(FAR_FIRST_8):
        j = (z + k) % NZ
        first_row = first_ref[first_slot + j] * (radial_rows // NRB)
        keep = (row_id >= first_row) & (col_id < count_ref[first_slot + j])
        masked = jnp.where(keep, radial_own[j].astype(jnp.float32), 0.0)
        masked_ref[i] = masked.astype(jnp.bfloat16)
    pl.semaphore_wait(barrier, NPLANE - 1 + NZ - 1)
    own = own_block(spec_ref, rows_ref, own_1)
    own.start()
    for part in range(len(SLOT_PARTS)):
        send_part(part, spec_ref, rows_ref, send_1, recv_1)
    own.wait()

    peers = list(z_peers())
    for part, spots in enumerate(SLOT_PARTS):
        wait_part(part, spec_ref, rows_ref, send_1, recv_1)
        for i in spots:
            rows = rows_ref[:, i].astype(jnp.float32).reshape(NPLANE * 8, radial_rows)
            coef = jnp.dot(
                rows.astype(jnp.bfloat16), masked_ref[i], preferred_element_type=jnp.float32
            ).astype(jnp.bfloat16)
            coef_ref[i] = coef
            cov = lax.dot_general(
                coef, coef, (((0,), (0,)), ((), ())), preferred_element_type=jnp.float32
            )
            if i < len(peers):
                _, there, pd = peers[i]
                given_ref[i] = cov.astype(jnp.bfloat16)
                remote(given_ref.at[i], taken_ref.at[there], send_2, recv_2, (pd, o)).start()
            else:
                part_ref[...] = cov
    wait_blocks(given_ref, taken_ref, send_2, recv_2, NZ - 1)
    cov = part_ref[...]
    for i in range(NZ - 1):
        cov = cov + taken_ref[i].astype(jnp.float32)

    cov_high, cov_low = split(cov, 2)
    basis_t = start_own[...]
    for step in range(ITERS):
        basis_t = orthonormal(times_cov(basis_t, cov_high, cov_low))
    eig_t = basis_t.astype(jnp.bfloat16)
    eigs_ref[NZ - 1] = eig_t
    for i, there, pd in peers:
        remote(
            eigs_ref.at[NZ - 1], eigs_ref.at[there], send_3.at[i], recv_3.at[there], (pd, o)
        ).start()

    for part in reversed(range(len(SLOT_PARTS))):
        for i in reversed(SLOT_PARTS[part]):
            if i < len(peers):
                remote(
                    eigs_ref.at[i], eigs_ref.at[i], send_3.at[i], recv_3.at[i], (peers[i][2], o)
                ).wait_recv()
            eig_t = eigs_ref[i]
            u_t = lax.dot_general(
                eig_t, masked_ref[i], (((1,), (1,)), ((), ())), preferred_element_type=jnp.float32
            ).astype(jnp.bfloat16)
            scores = lax.dot_general(
                coef_ref[i], eig_t, (((1,), (1,)), ((), ())), preferred_element_type=jnp.float32
            ).astype(jnp.bfloat16)
            profile = jnp.dot(scores, u_t, preferred_element_type=jnp.float32)
            prof_ref[:, i] = profile.reshape(NPLANE, 8, radial_rows).astype(jnp.bfloat16)
        send_part(part, prof_ref, out_ref, send_4, recv_4)
    own = own_block(prof_ref, out_ref, own_4)
    own.start()
    for i, _, pd in peers:
        remote(
            eigs_ref.at[NZ - 1], eigs_ref.at[i], send_3.at[i], recv_3.at[i], (pd, o)
        ).wait_send()
    own.wait()
    for part in reversed(range(len(SLOT_PARTS))):
        wait_part(part, prof_ref, out_ref, send_4, recv_4)


def on_device(polar_images, radial_basis, radial_start, radial_count, order_of_slot, start_block):
    particles, radial_rows, angles = polar_images.shape
    rank, width = start_block.shape[1:]
    slots = order_of_slot.shape[0]
    blocks = (NPLANE, NZ, 2 * particles, radial_rows)
    vmem = pl.BlockSpec(memory_space=pltpu.VMEM)
    smem = pl.BlockSpec(memory_space=pltpu.SMEM)
    anywhere = pl.BlockSpec(memory_space=pl.ANY)
    table, mine = pl.pallas_call(
        whole_kernel,
        out_shape=(
            jax.ShapeDtypeStruct((2 * slots, angles), jnp.bfloat16),
            jax.ShapeDtypeStruct(blocks, jnp.bfloat16),
        ),
        in_specs=[vmem, anywhere, smem, smem, vmem, anywhere],
        out_specs=(vmem, vmem),
        scratch_shapes=[
            pltpu.VMEM((slots * 2 * particles, radial_rows), jnp.float32),
            pltpu.VMEM(blocks, jnp.bfloat16),
            pltpu.VMEM(blocks, jnp.bfloat16),
            pltpu.VMEM((NZ, radial_rows, width), jnp.bfloat16),
            pltpu.VMEM((NZ, radial_rows, width), jnp.bfloat16),
            pltpu.VMEM((NZ, NPLANE * 2 * particles, width), jnp.bfloat16),
            pltpu.VMEM((width, width), jnp.float32),
            pltpu.VMEM((NZ, width, width), jnp.bfloat16),
            pltpu.VMEM((NZ, width, width), jnp.bfloat16),
            pltpu.VMEM((NZ, rank, width), jnp.bfloat16),
            pltpu.VMEM(blocks, jnp.bfloat16),
            pltpu.VMEM((rank, width), jnp.float32),
            *[pltpu.SemaphoreType.DMA((len(SLOT_PARTS),))] * 4,
            *[pltpu.SemaphoreType.DMA((NZ - 1,))] * 2,
            *[pltpu.SemaphoreType.DMA] * 6,
        ],
        compiler_params=pltpu.CompilerParams(collective_id=0, has_side_effects=True),
        name="whole",
    )(
        polar_images,
        radial_basis,
        radial_start,
        radial_count,
        order_of_slot.reshape(2, slots // 2),
        start_block,
    )
    mine = mine.reshape(slots, 2, particles, radial_rows)
    table = table.reshape(2, slots, angles)
    denoised = jnp.einsum("scpr,cst->prt", mine, table, preferred_element_type=jnp.float32)
    return denoised.astype(jnp.bfloat16)


def solution(mesh):
    placed = (
        P(("dom", "ord"), None, None),
        P("ord", None, None),
        P("ord"),
        P("ord"),
        P(),
        P("ord", None, None),
    )
    return jax.shard_map(
        on_device,
        mesh=mesh,
        in_specs=placed,
        out_specs=P(("dom", "ord"), None, None),
        check_vma=False,
    )
```

```python
import math

import jax
import jax.numpy as jnp
from jax import lax
from jax.experimental import pallas as pl
from jax.experimental.pallas import tpu as pltpu
from jax.sharding import PartitionSpec as P

NRB = 8
ITERS = 4
NZ, NY, NX = 8, 4, 4
NDOM = NZ * NY * NX
NPLANE = 2 * NY * NX
MESH = pl.DeviceIdType.MESH


FAR_FIRST_8 = (4, 3, 5, 2, 6, 1, 7, 0)
FAR_FIRST_4 = (2, 1, 3, 0)
SLOT_PARTS = ((0, 1), (2, 3), (4, 5), (6, 7))


def dot32(a, b, dims):
    return lax.dot_general(
        a, b, (dims, ((), ())), precision=lax.Precision.HIGHEST, preferred_element_type=jnp.float32
    )


def split(value, pieces):
    out = []
    for _ in range(pieces):
        piece = value.astype(jnp.bfloat16)
        value = value - piece.astype(jnp.float32)
        out.append(piece)
    return out


def times_cov(basis_t, cov_high, cov_low):
    rank = basis_t.shape[0]
    high, low = split(basis_t, 2)
    both = jnp.dot(
        jnp.concatenate([high, low], axis=0), cov_high, preferred_element_type=jnp.float32
    )
    rest = jnp.dot(high, cov_low, preferred_element_type=jnp.float32)
    return both[:rank] + (both[rank:] + rest)


def fold(cov):
    lane = lax.broadcasted_iota(jnp.int32, (32, 128), 1)
    second = jnp.where(lane < 32, pltpu.roll(cov[96:], 32, 1), cov[32:64])
    third = jnp.where(lane[:16] < 64, pltpu.roll(cov[80:96], 64, 1), cov[64:80])
    return jnp.concatenate([cov[:32], second, third], axis=0)


def unfold(folded):
    second, third = folded[32:64], folded[64:]
    upper = jnp.concatenate(
        [folded[:32], second, third, pltpu.roll(third, 64, 1), pltpu.roll(second, 96, 1)], axis=0
    )
    row_block = lax.broadcasted_iota(jnp.int32, (128, 128), 0) // 32
    lane_block = lax.broadcasted_iota(jnp.int32, (128, 128), 1) // 32
    return jnp.where(row_block > lane_block, upper.T, upper)


def orthonormal(image_t):
    rank, width = image_t.shape
    gram = dot32(image_t, image_t, ((1,), (1,)))
    lane_block = lax.broadcasted_iota(jnp.int32, (rank, rank * width), 1) // width
    spread = lane_block == lax.broadcasted_iota(jnp.int32, (rank, rank * width), 0)
    pieces = jnp.concatenate(split(gram, 3), axis=0)
    wide = jnp.dot(
        pieces, jnp.where(spread, 1.0, 0.0).astype(jnp.bfloat16), preferred_element_type=jnp.float32
    )
    wide = wide[:rank] + wide[rank : 2 * rank] + wide[2 * rank :]
    cols = [wide[:, j * width : (j + 1) * width] for j in range(rank)]
    row_id = lax.broadcasted_iota(jnp.int32, (rank, width), 0)
    pivots = jnp.ones((rank, width), jnp.float32)
    out = image_t
    for j in range(rank):
        pivot = jnp.broadcast_to(cols[j][j : j + 1, :], (rank, width))
        pivots = jnp.where(row_id == j, pivot, pivots)
        factor = jnp.where(row_id > j, cols[j] / pivot, 0.0)
        for k in range(j + 1, rank):
            cols[k] = cols[k] - factor * cols[k][j : j + 1, :]
        out = out - factor * out[j : j + 1, :]
    return out / jnp.sqrt(pivots)


def place():
    d = lax.axis_index("dom")
    return d, lax.axis_index("ord"), d // (NY * NX), (d // NX) % NY, d % NX


def z_peers():
    d, o, z, y, x = place()
    for i, k in enumerate(FAR_FIRST_8[:-1]):
        pd = (z + k) % NZ * (NY * NX) + y * NX + x
        yield i, FAR_FIRST_8.index((NZ - k) % NZ), pd


def plane_peers():
    d, o, z, y, x = place()
    at_y = [(y + k) % NY * NX for k in range(NY)]
    at_x = [(x + k) % NX for k in range(NX)]
    for dy in FAR_FIRST_4:
        for dx in FAR_FIRST_4:
            m = at_y[dy] + at_x[dx]
            for po in (1 - o, o) if (dy, dx) != (0, 0) else (1 - o,):
                yield po * (NY * NX) + m, z * (NY * NX) + m, po


def remote(src_ref, dst_ref, send_sem, recv_sem, device):
    return pltpu.make_async_remote_copy(
        src_ref=src_ref,
        dst_ref=dst_ref,
        send_sem=send_sem,
        recv_sem=recv_sem,
        device_id=device,
        device_id_type=MESH,
    )


def wait_blocks(src_ref, dst_ref, send_sem, recv_sem, blocks):
    d, o = place()[:2]
    most = pl.ds(0, blocks)
    everything = remote(src_ref.at[most], dst_ref.at[most], send_sem, recv_sem, (d, 1 - o))
    everything.wait_send()
    everything.wait_recv()


def own_block(src_ref, dst_ref, own_sem):
    d, o, z, y, x = place()
    mine = o * (NY * NX) + y * NX + x
    return pltpu.make_async_copy(src_ref.at[mine], dst_ref.at[mine], own_sem)


def send_part(part, src_ref, dst_ref, send_sem, recv_sem):
    d, o, z, y, x = place()
    mine = o * (NY * NX) + y * NX + x
    span = pl.ds(SLOT_PARTS[part][0], len(SLOT_PARTS[part]))
    for index, pd, po in plane_peers():
        remote(
            src_ref.at[index, span],
            dst_ref.at[mine, span],
            send_sem.at[part],
            recv_sem.at[part],
            (pd, po),
        ).start()


def wait_part(part, src_ref, dst_ref, send_sem, recv_sem):
    span = pl.ds(SLOT_PARTS[part][0], len(SLOT_PARTS[part]))
    wait_blocks(
        src_ref.at[:, span], dst_ref.at[:, span], send_sem.at[part], recv_sem.at[part], NPLANE - 1
    )


def fill_table(order_ref, table_ref):
    angles = table_ref.shape[1]
    weight = math.sqrt(2.0 / angles)
    z = place()[2]
    row_id = lax.broadcasted_iota(jnp.int32, (128, 128), 0)
    lane = lax.broadcasted_iota(jnp.int32, (128, 128), 1)
    spot = row_id & (NZ - 1)
    step = (spot + 1) >> 1
    offset = NZ // 2 + jnp.where((spot & 1) == 1, -step, step)
    chosen = lane == row_id - spot + ((z + offset) & (NZ - 1))
    chosen = jnp.where(chosen, 1.0, 0.0).astype(jnp.bfloat16)
    for half in range(2):
        row = order_ref[half : half + 1, :].astype(jnp.float32)
        k = lax.dot_general(
            chosen,
            jnp.broadcast_to(row, (128, 128)).astype(jnp.bfloat16),
            (((1,), (1,)), ((), ())),
            preferred_element_type=jnp.float32,
        ).astype(jnp.int32)
        turn = (k * lane) & (angles - 1)
        quarter = (turn + angles // 8) >> 7
        angle = (turn - quarter * (angles // 4)).astype(jnp.float32) * (2.0 * math.pi / angles)
        sq = angle * angle
        cos = 1.0 + sq * (-1 / 2 + sq * (1 / 24 + sq * (-1 / 720 + sq * (1 / 40320))))
        sin = angle * (1.0 + sq * (-1 / 6 + sq * (1 / 120 + sq * (-1 / 5040 + sq * (1 / 362880)))))
        cos = cos * weight
        sin = sin * weight
        for b in range(angles // 128):
            quadrant = (quarter + b * k) & 3
            odd = (quadrant & 1) == 1
            upper = quadrant >= 2
            even_sign = jnp.where(upper, -1.0, 1.0)
            real = jnp.where(odd, -sin, cos) * even_sign
            imag = jnp.where(odd, -cos, -sin) * even_sign
            span = slice(128 * b, 128 * (b + 1))
            table_ref[128 * half : 128 * (half + 1), span] = real.astype(jnp.bfloat16)
            table_ref[256 + 128 * half : 256 + 128 * (half + 1), span] = imag.astype(jnp.bfloat16)


def fill_spectrum(table_ref, images_ref, wide_ref):
    slots = table_ref.shape[0] // 2
    for p in range(0, images_ref.shape[0], 2):
        pair = images_ref[p : p + 2].reshape(2 * images_ref.shape[1], images_ref.shape[2])
        for c in range(2):
            part = lax.dot_general(
                table_ref[slots * c : slots * (c + 1), :],
                pair,
                (((1,), (1,)), ((), ())),
                preferred_element_type=jnp.float32,
            )
            wide_ref[pl.ds(4 * c + p, slots, stride=8), :] = part[:, :128]
            wide_ref[pl.ds(4 * c + p + 1, slots, stride=8), :] = part[:, 128:]


def whole_kernel(
    images_ref,
    radial_ref,
    first_ref,
    count_ref,
    order_ref,
    start_ref,
    table_ref,
    out_ref,
    wide_ref,
    spec_ref,
    rows_ref,
    radial_own,
    masked_ref,
    coef_ref,
    part_ref,
    given_ref,
    taken_ref,
    eigs_ref,
    prof_ref,
    start_own,
    send_1,
    recv_1,
    send_4,
    recv_4,
    send_3,
    recv_3,
    send_2,
    recv_2,
    own_1,
    own_4,
    load_1,
    load_2,
):
    d, o, z, y, x = place()
    first_slot = (y * NX + x) * NZ
    barrier = pltpu.get_barrier_semaphore()
    for _, _, pd in z_peers():
        pl.semaphore_signal(barrier, inc=1, device_id=(pd, o), device_id_type=MESH)
    for _, pd, po in plane_peers():
        pl.semaphore_signal(barrier, inc=1, device_id=(pd, po), device_id_type=MESH)
    radial_load = pltpu.make_async_copy(radial_ref.at[pl.ds(first_slot, NZ)], radial_own, load_1)
    start_load = pltpu.make_async_copy(start_ref.at[first_slot + z], start_own, load_2)
    radial_load.start()
    start_load.start()
    fill_table(order_ref, table_ref)
    fill_spectrum(table_ref, images_ref, wide_ref)
    spec_ref[...] = wide_ref[...].reshape(spec_ref.shape).astype(jnp.bfloat16)
    radial_load.wait()
    start_load.wait()
    radial_rows, width = masked_ref.shape[1:]
    row_id = lax.broadcasted_iota(jnp.int32, (radial_rows, width), 0)
    col_id = lax.broadcasted_iota(jnp.int32, (radial_rows, width), 1)
    for i, k in enumerate(FAR_FIRST_8):
        j = (z + k) % NZ
        first_row = first_ref[first_slot + j] * (radial_rows // NRB)
        keep = (row_id >= first_row) & (col_id < count_ref[first_slot + j])
        masked = jnp.where(keep, radial_own[j].astype(jnp.float32), 0.0)
        masked_ref[i] = masked.astype(jnp.bfloat16)
    pl.semaphore_wait(barrier, NPLANE - 1 + NZ - 1)
    own = own_block(spec_ref, rows_ref, own_1)
    own.start()
    for part in range(len(SLOT_PARTS)):
        send_part(part, spec_ref, rows_ref, send_1, recv_1)
    own.wait()

    peers = list(z_peers())
    for part, spots in enumerate(SLOT_PARTS):
        wait_part(part, spec_ref, rows_ref, send_1, recv_1)
        for i in spots:
            rows = rows_ref[:, i].astype(jnp.float32).reshape(NPLANE * 8, radial_rows)
            coef = jnp.dot(
                rows.astype(jnp.bfloat16), masked_ref[i], preferred_element_type=jnp.float32
            ).astype(jnp.bfloat16)
            coef_ref[i] = coef
            cov = fold(
                lax.dot_general(
                    coef, coef, (((0,), (0,)), ((), ())), preferred_element_type=jnp.float32
                )
            )
            if i < len(peers):
                _, there, pd = peers[i]
                given_ref[i] = cov.astype(jnp.bfloat16)
                remote(given_ref.at[i], taken_ref.at[there], send_2, recv_2, (pd, o)).start()
            else:
                part_ref[...] = cov
    wait_blocks(given_ref, taken_ref, send_2, recv_2, NZ - 1)
    cov = part_ref[...]
    for i in range(NZ - 1):
        cov = cov + taken_ref[i].astype(jnp.float32)

    cov_high, cov_low = split(unfold(cov), 2)
    basis_t = start_own[...]
    for step in range(ITERS):
        basis_t = orthonormal(times_cov(basis_t, cov_high, cov_low))
    eig_t = basis_t.astype(jnp.bfloat16)
    eigs_ref[NZ - 1] = eig_t
    for i, there, pd in peers:
        remote(
            eigs_ref.at[NZ - 1], eigs_ref.at[there], send_3.at[i], recv_3.at[there], (pd, o)
        ).start()

    for part in reversed(range(len(SLOT_PARTS))):
        for i in reversed(SLOT_PARTS[part]):
            if i < len(peers):
                remote(
                    eigs_ref.at[i], eigs_ref.at[i], send_3.at[i], recv_3.at[i], (peers[i][2], o)
                ).wait_recv()
            eig_t = eigs_ref[i]
            u_t = lax.dot_general(
                eig_t, masked_ref[i], (((1,), (1,)), ((), ())), preferred_element_type=jnp.float32
            ).astype(jnp.bfloat16)
            scores = lax.dot_general(
                coef_ref[i], eig_t, (((1,), (1,)), ((), ())), preferred_element_type=jnp.float32
            ).astype(jnp.bfloat16)
            profile = jnp.dot(scores, u_t, preferred_element_type=jnp.float32)
            prof_ref[:, i] = profile.reshape(NPLANE, 8, radial_rows).astype(jnp.bfloat16)
        send_part(part, prof_ref, out_ref, send_4, recv_4)
    own = own_block(prof_ref, out_ref, own_4)
    own.start()
    for i, _, pd in peers:
        remote(
            eigs_ref.at[NZ - 1], eigs_ref.at[i], send_3.at[i], recv_3.at[i], (pd, o)
        ).wait_send()
    own.wait()
    for part in reversed(range(len(SLOT_PARTS))):
        wait_part(part, prof_ref, out_ref, send_4, recv_4)


def on_device(polar_images, radial_basis, radial_start, radial_count, order_of_slot, start_block):
    particles, radial_rows, angles = polar_images.shape
    rank, width = start_block.shape[1:]
    slots = order_of_slot.shape[0]
    blocks = (NPLANE, NZ, 2 * particles, radial_rows)
    vmem = pl.BlockSpec(memory_space=pltpu.VMEM)
    smem = pl.BlockSpec(memory_space=pltpu.SMEM)
    anywhere = pl.BlockSpec(memory_space=pl.ANY)
    table, mine = pl.pallas_call(
        whole_kernel,
        out_shape=(
            jax.ShapeDtypeStruct((2 * slots, angles), jnp.bfloat16),
            jax.ShapeDtypeStruct(blocks, jnp.bfloat16),
        ),
        in_specs=[vmem, anywhere, smem, smem, vmem, anywhere],
        out_specs=(vmem, vmem),
        scratch_shapes=[
            pltpu.VMEM((slots * 2 * particles, radial_rows), jnp.float32),
            pltpu.VMEM(blocks, jnp.bfloat16),
            pltpu.VMEM(blocks, jnp.bfloat16),
            pltpu.VMEM((NZ, radial_rows, width), jnp.bfloat16),
            pltpu.VMEM((NZ, radial_rows, width), jnp.bfloat16),
            pltpu.VMEM((NZ, NPLANE * 2 * particles, width), jnp.bfloat16),
            pltpu.VMEM((80, width), jnp.float32),
            pltpu.VMEM((NZ, 80, width), jnp.bfloat16),
            pltpu.VMEM((NZ, 80, width), jnp.bfloat16),
            pltpu.VMEM((NZ, rank, width), jnp.bfloat16),
            pltpu.VMEM(blocks, jnp.bfloat16),
            pltpu.VMEM((rank, width), jnp.float32),
            *[pltpu.SemaphoreType.DMA((len(SLOT_PARTS),))] * 4,
            *[pltpu.SemaphoreType.DMA((NZ - 1,))] * 2,
            *[pltpu.SemaphoreType.DMA] * 6,
        ],
        compiler_params=pltpu.CompilerParams(collective_id=0, has_side_effects=True),
        name="whole",
    )(
        polar_images,
        radial_basis,
        radial_start,
        radial_count,
        order_of_slot.reshape(2, slots // 2),
        start_block,
    )
    mine = mine.reshape(slots, 2, particles, radial_rows)
    table = table.reshape(2, slots, angles)
    denoised = jnp.einsum("scpr,cst->prt", mine, table, preferred_element_type=jnp.float32)
    return denoised.astype(jnp.bfloat16)


def solution(mesh):
    placed = (
        P(("dom", "ord"), None, None),
        P("ord", None, None),
        P("ord"),
        P("ord"),
        P(),
        P("ord", None, None),
    )
    return jax.shard_map(
        on_device,
        mesh=mesh,
        in_specs=placed,
        out_specs=P(("dom", "ord"), None, None),
        check_vma=False,
    )
```

```python
import math

import jax
import jax.numpy as jnp
from jax import lax
from jax.experimental import pallas as pl
from jax.experimental.pallas import tpu as pltpu
from jax.sharding import PartitionSpec as P

NRB = 8
ITERS = 4
NZ, NY, NX = 8, 4, 4
NDOM = NZ * NY * NX
NPLANE = 2 * NY * NX
MESH = pl.DeviceIdType.MESH


FAR_FIRST_8 = (4, 3, 5, 2, 6, 1, 7, 0)
FAR_FIRST_4 = (2, 1, 3, 0)
SLOT_PARTS = ((0, 1), (2, 3), (4, 5), (6, 7))


def dot32(a, b, dims):
    return lax.dot_general(
        a, b, (dims, ((), ())), precision=lax.Precision.HIGHEST, preferred_element_type=jnp.float32
    )


def split(value, pieces):
    out = []
    for _ in range(pieces):
        piece = value.astype(jnp.bfloat16)
        value = value - piece.astype(jnp.float32)
        out.append(piece)
    return out


def times_cov(basis_t, cov_high, cov_low):
    rank = basis_t.shape[0]
    high, low = split(basis_t, 2)
    both = jnp.dot(
        jnp.concatenate([high, low], axis=0), cov_high, preferred_element_type=jnp.float32
    )
    rest = jnp.dot(high, cov_low, preferred_element_type=jnp.float32)
    return both[:rank] + (both[rank:] + rest)


def fold(cov):
    lane = lax.broadcasted_iota(jnp.int32, (32, 128), 1)
    second = jnp.where(lane < 32, pltpu.roll(cov[96:], 32, 1), cov[32:64])
    third = jnp.where(lane[:16] < 64, pltpu.roll(cov[80:96], 64, 1), cov[64:80])
    return jnp.concatenate([cov[:32], second, third], axis=0)


def unfold(folded):
    second, third = folded[32:64], folded[64:]
    upper = jnp.concatenate(
        [folded[:32], second, third, pltpu.roll(third, 64, 1), pltpu.roll(second, 96, 1)], axis=0
    )
    row_block = lax.broadcasted_iota(jnp.int32, (128, 128), 0) // 32
    lane_block = lax.broadcasted_iota(jnp.int32, (128, 128), 1) // 32
    return jnp.where(row_block > lane_block, upper.T, upper)


def orthonormal(image_t):
    rank, width = image_t.shape
    gram = dot32(image_t, image_t, ((1,), (1,)))
    lane_block = lax.broadcasted_iota(jnp.int32, (rank, rank * width), 1) // width
    spread = lane_block == lax.broadcasted_iota(jnp.int32, (rank, rank * width), 0)
    pieces = jnp.concatenate(split(gram, 3), axis=0)
    wide = jnp.dot(
        pieces, jnp.where(spread, 1.0, 0.0).astype(jnp.bfloat16), preferred_element_type=jnp.float32
    )
    wide = wide[:rank] + wide[rank : 2 * rank] + wide[2 * rank :]
    cols = [wide[:, j * width : (j + 1) * width] for j in range(rank)]
    row_id = lax.broadcasted_iota(jnp.int32, (rank, width), 0)
    pivots = jnp.ones((rank, width), jnp.float32)
    out = image_t
    for j in range(rank):
        pivot = jnp.broadcast_to(cols[j][j : j + 1, :], (rank, width))
        pivots = jnp.where(row_id == j, pivot, pivots)
        factor = jnp.where(row_id > j, cols[j] / pivot, 0.0)
        for k in range(j + 1, rank):
            cols[k] = cols[k] - factor * cols[k][j : j + 1, :]
        out = out - factor * out[j : j + 1, :]
    return out / jnp.sqrt(pivots)


def place():
    d = lax.axis_index("dom")
    return d, lax.axis_index("ord"), d // (NY * NX), (d // NX) % NY, d % NX


def z_peers():
    d, o, z, y, x = place()
    for i, k in enumerate(FAR_FIRST_8[:-1]):
        pd = (z + k) % NZ * (NY * NX) + y * NX + x
        yield i, FAR_FIRST_8.index((NZ - k) % NZ), pd


def plane_peers():
    d, o, z, y, x = place()
    at_y = [(y + k) % NY * NX for k in range(NY)]
    at_x = [(x + k) % NX for k in range(NX)]
    for dy in FAR_FIRST_4:
        for dx in FAR_FIRST_4:
            m = at_y[dy] + at_x[dx]
            for po in (1 - o, o) if (dy, dx) != (0, 0) else (1 - o,):
                yield po * (NY * NX) + m, z * (NY * NX) + m, po


def remote(src_ref, dst_ref, send_sem, recv_sem, device):
    return pltpu.make_async_remote_copy(
        src_ref=src_ref,
        dst_ref=dst_ref,
        send_sem=send_sem,
        recv_sem=recv_sem,
        device_id=device,
        device_id_type=MESH,
    )


def wait_blocks(src_ref, dst_ref, send_sem, recv_sem, blocks):
    d, o = place()[:2]
    most = pl.ds(0, blocks)
    everything = remote(src_ref.at[most], dst_ref.at[most], send_sem, recv_sem, (d, 1 - o))
    everything.wait_send()
    everything.wait_recv()


def own_block(src_ref, dst_ref, own_sem):
    d, o, z, y, x = place()
    mine = o * (NY * NX) + y * NX + x
    return pltpu.make_async_copy(src_ref.at[mine], dst_ref.at[mine], own_sem)


def send_part(part, src_ref, dst_ref, send_sem, recv_sem):
    d, o, z, y, x = place()
    mine = o * (NY * NX) + y * NX + x
    span = pl.ds(SLOT_PARTS[part][0], len(SLOT_PARTS[part]))
    for index, pd, po in plane_peers():
        remote(
            src_ref.at[index, span],
            dst_ref.at[mine, span],
            send_sem.at[part],
            recv_sem.at[part],
            (pd, po),
        ).start()


def wait_part(part, src_ref, dst_ref, send_sem, recv_sem):
    span = pl.ds(SLOT_PARTS[part][0], len(SLOT_PARTS[part]))
    wait_blocks(
        src_ref.at[:, span], dst_ref.at[:, span], send_sem.at[part], recv_sem.at[part], NPLANE - 1
    )


def fill_table(order_ref, table_ref):
    angles = table_ref.shape[1]
    weight = math.sqrt(2.0 / angles)
    z = place()[2]
    row_id = lax.broadcasted_iota(jnp.int32, (128, 128), 0)
    lane = lax.broadcasted_iota(jnp.int32, (128, 128), 1)
    spot = row_id & (NZ - 1)
    step = (spot + 1) >> 1
    offset = NZ // 2 + jnp.where((spot & 1) == 1, -step, step)
    chosen = lane == row_id - spot + ((z + offset) & (NZ - 1))
    chosen = jnp.where(chosen, 1.0, 0.0).astype(jnp.bfloat16)
    for half in range(2):
        row = order_ref[half : half + 1, :].astype(jnp.float32)
        k = lax.dot_general(
            chosen,
            jnp.broadcast_to(row, (128, 128)).astype(jnp.bfloat16),
            (((1,), (1,)), ((), ())),
            preferred_element_type=jnp.float32,
        ).astype(jnp.int32)
        turn = (k * lane) & (angles - 1)
        quarter = (turn + angles // 8) >> 7
        angle = (turn - quarter * (angles // 4)).astype(jnp.float32) * (2.0 * math.pi / angles)
        sq = angle * angle
        cos = 1.0 + sq * (-1 / 2 + sq * (1 / 24 + sq * (-1 / 720 + sq * (1 / 40320))))
        sin = angle * (1.0 + sq * (-1 / 6 + sq * (1 / 120 + sq * (-1 / 5040 + sq * (1 / 362880)))))
        cos = cos * weight
        sin = sin * weight
        for b in range(angles // 128):
            quadrant = (quarter + b * k) & 3
            odd = (quadrant & 1) == 1
            upper = quadrant >= 2
            even_sign = jnp.where(upper, -1.0, 1.0)
            real = jnp.where(odd, -sin, cos) * even_sign
            imag = jnp.where(odd, -cos, -sin) * even_sign
            span = slice(128 * b, 128 * (b + 1))
            table_ref[128 * half : 128 * (half + 1), span] = real.astype(jnp.bfloat16)
            table_ref[256 + 128 * half : 256 + 128 * (half + 1), span] = imag.astype(jnp.bfloat16)


def fill_spectrum(table_ref, images_ref, wide_ref):
    slots = table_ref.shape[0] // 2
    for p in range(0, images_ref.shape[0], 2):
        pair = images_ref[p : p + 2].reshape(2 * images_ref.shape[1], images_ref.shape[2])
        for c in range(2):
            part = lax.dot_general(
                table_ref[slots * c : slots * (c + 1), :],
                pair,
                (((1,), (1,)), ((), ())),
                preferred_element_type=jnp.float32,
            )
            wide_ref[pl.ds(4 * c + p, slots, stride=8), :] = part[:, :128]
            wide_ref[pl.ds(4 * c + p + 1, slots, stride=8), :] = part[:, 128:]


def whole_kernel(
    images_ref,
    radial_ref,
    first_ref,
    count_ref,
    order_ref,
    start_ref,
    table_out,
    out_ref,
    table_ref,
    back_ref,
    wide_ref,
    spec_ref,
    rows_ref,
    radial_own,
    masked_ref,
    coef_ref,
    part_ref,
    given_ref,
    taken_ref,
    eigs_ref,
    prof_ref,
    start_own,
    send_1,
    recv_1,
    send_4,
    recv_4,
    send_3,
    recv_3,
    send_2,
    recv_2,
    own_1,
    own_4,
    load_1,
    load_2,
    store_1,
):
    d, o, z, y, x = place()
    first_slot = (y * NX + x) * NZ
    barrier = pltpu.get_barrier_semaphore()
    for _, _, pd in z_peers():
        pl.semaphore_signal(barrier, inc=1, device_id=(pd, o), device_id_type=MESH)
    for _, pd, po in plane_peers():
        pl.semaphore_signal(barrier, inc=1, device_id=(pd, po), device_id_type=MESH)
    radial_load = pltpu.make_async_copy(radial_ref.at[pl.ds(first_slot, NZ)], radial_own, load_1)
    start_load = pltpu.make_async_copy(start_ref.at[first_slot + z], start_own, load_2)
    radial_load.start()
    start_load.start()
    fill_table(order_ref, table_ref)
    table_store = pltpu.make_async_copy(table_ref, table_out, store_1)
    table_store.start()
    fill_spectrum(table_ref, images_ref, wide_ref)
    spec_ref[...] = wide_ref[...].reshape(spec_ref.shape).astype(jnp.bfloat16)
    radial_load.wait()
    start_load.wait()
    radial_rows, width = masked_ref.shape[1:]
    row_id = lax.broadcasted_iota(jnp.int32, (radial_rows, width), 0)
    col_id = lax.broadcasted_iota(jnp.int32, (radial_rows, width), 1)
    for i, k in enumerate(FAR_FIRST_8):
        j = (z + k) % NZ
        first_row = first_ref[first_slot + j] * (radial_rows // NRB)
        keep = (row_id >= first_row) & (col_id < count_ref[first_slot + j])
        masked = jnp.where(keep, radial_own[j].astype(jnp.float32), 0.0)
        masked_ref[i] = masked.astype(jnp.bfloat16)
    pl.semaphore_wait(barrier, NPLANE - 1 + NZ - 1)
    own = own_block(spec_ref, rows_ref, own_1)
    own.start()
    for part in range(len(SLOT_PARTS)):
        send_part(part, spec_ref, rows_ref, send_1, recv_1)
    own.wait()

    peers = list(z_peers())
    for part, spots in enumerate(SLOT_PARTS):
        wait_part(part, spec_ref, rows_ref, send_1, recv_1)
        for i in spots:
            rows = rows_ref[:, i].astype(jnp.float32).reshape(NPLANE * 8, radial_rows)
            coef = jnp.dot(
                rows.astype(jnp.bfloat16), masked_ref[i], preferred_element_type=jnp.float32
            ).astype(jnp.bfloat16)
            coef_ref[i] = coef
            cov = fold(
                lax.dot_general(
                    coef, coef, (((0,), (0,)), ((), ())), preferred_element_type=jnp.float32
                )
            )
            if i < len(peers):
                _, there, pd = peers[i]
                given_ref[i] = cov.astype(jnp.bfloat16)
                remote(given_ref.at[i], taken_ref.at[there], send_2, recv_2, (pd, o)).start()
            else:
                part_ref[...] = cov
    wait_blocks(given_ref, taken_ref, send_2, recv_2, NZ - 1)
    cov = part_ref[...]
    for i in range(NZ - 1):
        cov = cov + taken_ref[i].astype(jnp.float32)

    cov_high, cov_low = split(unfold(cov), 2)
    basis_t = start_own[...]
    for step in range(ITERS):
        basis_t = orthonormal(times_cov(basis_t, cov_high, cov_low))
    eig_t = basis_t.astype(jnp.bfloat16)
    eigs_ref[NZ - 1] = eig_t
    for i, there, pd in peers:
        remote(
            eigs_ref.at[NZ - 1], eigs_ref.at[there], send_3.at[i], recv_3.at[there], (pd, o)
        ).start()

    for part in reversed(range(len(SLOT_PARTS))):
        for i in reversed(SLOT_PARTS[part]):
            if i < len(peers):
                remote(
                    eigs_ref.at[i], eigs_ref.at[i], send_3.at[i], recv_3.at[i], (peers[i][2], o)
                ).wait_recv()
            eig_t = eigs_ref[i]
            u_t = lax.dot_general(
                eig_t, masked_ref[i], (((1,), (1,)), ((), ())), preferred_element_type=jnp.float32
            ).astype(jnp.bfloat16)
            scores = lax.dot_general(
                coef_ref[i], eig_t, (((1,), (1,)), ((), ())), preferred_element_type=jnp.float32
            ).astype(jnp.bfloat16)
            profile = jnp.dot(scores, u_t, preferred_element_type=jnp.float32)
            prof_ref[:, i] = profile.reshape(NPLANE, 8, radial_rows).astype(jnp.bfloat16)
        send_part(part, prof_ref, back_ref, send_4, recv_4)
    own = own_block(prof_ref, back_ref, own_4)
    own.start()
    for i, _, pd in peers:
        remote(
            eigs_ref.at[NZ - 1], eigs_ref.at[i], send_3.at[i], recv_3.at[i], (pd, o)
        ).wait_send()
    own.wait()

    by_slot = wide_ref.reshape(*back_ref.shape)
    for part in reversed(range(len(SLOT_PARTS))):
        wait_part(part, prof_ref, back_ref, send_4, recv_4)
        for i in SLOT_PARTS[part]:
            by_slot[:, i] = back_ref[:, i].astype(jnp.float32)
    slots = NPLANE * NZ
    for p in range(out_ref.shape[0]):
        for c in range(2):
            ordered = wide_ref[pl.ds(4 * c + p, slots, stride=8), :]
            out_ref[p, slots * c : slots * (c + 1), :] = ordered.astype(jnp.bfloat16)
    table_store.wait()


def on_device(polar_images, radial_basis, radial_start, radial_count, order_of_slot, start_block):
    particles, radial_rows, angles = polar_images.shape
    rank, width = start_block.shape[1:]
    slots = order_of_slot.shape[0]
    blocks = (NPLANE, NZ, 2 * particles, radial_rows)
    vmem = pl.BlockSpec(memory_space=pltpu.VMEM)
    smem = pl.BlockSpec(memory_space=pltpu.SMEM)
    anywhere = pl.BlockSpec(memory_space=pl.ANY)
    table, mine = pl.pallas_call(
        whole_kernel,
        out_shape=(
            jax.ShapeDtypeStruct((2 * slots, angles), jnp.bfloat16),
            jax.ShapeDtypeStruct((particles, 2 * slots, radial_rows), jnp.bfloat16),
        ),
        in_specs=[vmem, anywhere, smem, smem, vmem, anywhere],
        out_specs=(anywhere, vmem),
        scratch_shapes=[
            pltpu.VMEM((2 * slots, angles), jnp.bfloat16),
            pltpu.VMEM(blocks, jnp.bfloat16),
            pltpu.VMEM((slots * 2 * particles, radial_rows), jnp.float32),
            pltpu.VMEM(blocks, jnp.bfloat16),
            pltpu.VMEM(blocks, jnp.bfloat16),
            pltpu.VMEM((NZ, radial_rows, width), jnp.bfloat16),
            pltpu.VMEM((NZ, radial_rows, width), jnp.bfloat16),
            pltpu.VMEM((NZ, NPLANE * 2 * particles, width), jnp.bfloat16),
            pltpu.VMEM((80, width), jnp.float32),
            pltpu.VMEM((NZ, 80, width), jnp.bfloat16),
            pltpu.VMEM((NZ, 80, width), jnp.bfloat16),
            pltpu.VMEM((NZ, rank, width), jnp.bfloat16),
            pltpu.VMEM(blocks, jnp.bfloat16),
            pltpu.VMEM((rank, width), jnp.float32),
            *[pltpu.SemaphoreType.DMA((len(SLOT_PARTS),))] * 4,
            *[pltpu.SemaphoreType.DMA((NZ - 1,))] * 2,
            *[pltpu.SemaphoreType.DMA] * 7,
        ],
        compiler_params=pltpu.CompilerParams(collective_id=0, has_side_effects=True),
        name="whole",
    )(
        polar_images,
        radial_basis,
        radial_start,
        radial_count,
        order_of_slot.reshape(2, slots // 2),
        start_block,
    )
    denoised = jnp.einsum("per,et->prt", mine, table, preferred_element_type=jnp.float32)
    return denoised.astype(jnp.bfloat16)


def solution(mesh):
    placed = (
        P(("dom", "ord"), None, None),
        P("ord", None, None),
        P("ord"),
        P("ord"),
        P(),
        P("ord", None, None),
    )
    return jax.shard_map(
        on_device,
        mesh=mesh,
        in_specs=placed,
        out_specs=P(("dom", "ord"), None, None),
        check_vma=False,
    )
```

```python
import math

import jax
import jax.numpy as jnp
from jax import lax
from jax.experimental import pallas as pl
from jax.experimental.pallas import tpu as pltpu
from jax.sharding import PartitionSpec as P

NRB = 8
ITERS = 4
NZ, NY, NX = 8, 4, 4
NDOM = NZ * NY * NX
NPLANE = 2 * NY * NX
MESH = pl.DeviceIdType.MESH


FAR_FIRST_8 = (4, 3, 5, 2, 6, 1, 7, 0)
FAR_FIRST_4 = (2, 1, 3, 0)
SLOT_PARTS = ((0, 1), (2, 3), (4, 5), (6, 7))


def dot32(a, b, dims):
    return lax.dot_general(
        a, b, (dims, ((), ())), precision=lax.Precision.HIGHEST, preferred_element_type=jnp.float32
    )


def split(value, pieces):
    out = []
    for _ in range(pieces):
        piece = value.astype(jnp.bfloat16)
        value = value - piece.astype(jnp.float32)
        out.append(piece)
    return out


def times_cov(basis_t, cov_high, cov_low):
    rank = basis_t.shape[0]
    high, low = split(basis_t, 2)
    both = jnp.dot(
        jnp.concatenate([high, low], axis=0), cov_high, preferred_element_type=jnp.float32
    )
    rest = jnp.dot(high, cov_low, preferred_element_type=jnp.float32)
    return both[:rank] + (both[rank:] + rest)


def fold(cov):
    lane = lax.broadcasted_iota(jnp.int32, (32, 128), 1)
    second = jnp.where(lane < 32, pltpu.roll(cov[96:], 32, 1), cov[32:64])
    third = jnp.where(lane[:16] < 64, pltpu.roll(cov[80:96], 64, 1), cov[64:80])
    return jnp.concatenate([cov[:32], second, third], axis=0)


def unfold(folded):
    second, third = folded[32:64], folded[64:]
    upper = jnp.concatenate(
        [folded[:32], second, third, pltpu.roll(third, 64, 1), pltpu.roll(second, 96, 1)], axis=0
    )
    row_block = lax.broadcasted_iota(jnp.int32, (128, 128), 0) // 32
    lane_block = lax.broadcasted_iota(jnp.int32, (128, 128), 1) // 32
    return jnp.where(row_block > lane_block, upper.T, upper)


def orthonormal(image_t):
    rank, width = image_t.shape
    gram = dot32(image_t, image_t, ((1,), (1,)))
    lane_block = lax.broadcasted_iota(jnp.int32, (rank, rank * width), 1) // width
    spread = lane_block == lax.broadcasted_iota(jnp.int32, (rank, rank * width), 0)
    pieces = jnp.concatenate(split(gram, 3), axis=0)
    wide = jnp.dot(
        pieces, jnp.where(spread, 1.0, 0.0).astype(jnp.bfloat16), preferred_element_type=jnp.float32
    )
    wide = wide[:rank] + wide[rank : 2 * rank] + wide[2 * rank :]
    cols = [wide[:, j * width : (j + 1) * width] for j in range(rank)]
    row_id = lax.broadcasted_iota(jnp.int32, (rank, width), 0)
    pivots = jnp.ones((rank, width), jnp.float32)
    out = image_t
    for j in range(rank):
        pivot = jnp.broadcast_to(cols[j][j : j + 1, :], (rank, width))
        pivots = jnp.where(row_id == j, pivot, pivots)
        factor = jnp.where(row_id > j, cols[j] / pivot, 0.0)
        for k in range(j + 1, rank):
            cols[k] = cols[k] - factor * cols[k][j : j + 1, :]
        out = out - factor * out[j : j + 1, :]
    return out / jnp.sqrt(pivots)


def place():
    d = lax.axis_index("dom")
    return d, lax.axis_index("ord"), d // (NY * NX), (d // NX) % NY, d % NX


def z_peers():
    d, o, z, y, x = place()
    for i, k in enumerate(FAR_FIRST_8[:-1]):
        pd = (z + k) % NZ * (NY * NX) + y * NX + x
        yield i, FAR_FIRST_8.index((NZ - k) % NZ), pd


def plane_peers():
    d, o, z, y, x = place()
    at_y = [(y + k) % NY * NX for k in range(NY)]
    at_x = [(x + k) % NX for k in range(NX)]
    for dy in FAR_FIRST_4:
        for dx in FAR_FIRST_4:
            m = at_y[dy] + at_x[dx]
            for po in (1 - o, o) if (dy, dx) != (0, 0) else (1 - o,):
                yield po * (NY * NX) + m, z * (NY * NX) + m, po


def remote(src_ref, dst_ref, send_sem, recv_sem, device):
    return pltpu.make_async_remote_copy(
        src_ref=src_ref,
        dst_ref=dst_ref,
        send_sem=send_sem,
        recv_sem=recv_sem,
        device_id=device,
        device_id_type=MESH,
    )


def wait_blocks(src_ref, dst_ref, send_sem, recv_sem, blocks):
    d, o = place()[:2]
    most = pl.ds(0, blocks)
    everything = remote(src_ref.at[most], dst_ref.at[most], send_sem, recv_sem, (d, 1 - o))
    everything.wait_send()
    everything.wait_recv()


def own_block(src_ref, dst_ref, own_sem):
    d, o, z, y, x = place()
    mine = o * (NY * NX) + y * NX + x
    return pltpu.make_async_copy(src_ref.at[mine], dst_ref.at[mine], own_sem)


def send_part(part, src_ref, dst_ref, send_sem, recv_sem):
    d, o, z, y, x = place()
    mine = o * (NY * NX) + y * NX + x
    span = pl.ds(SLOT_PARTS[part][0], len(SLOT_PARTS[part]))
    for index, pd, po in plane_peers():
        remote(
            src_ref.at[index, span],
            dst_ref.at[mine, span],
            send_sem.at[part],
            recv_sem.at[part],
            (pd, po),
        ).start()


def wait_part(part, src_ref, dst_ref, send_sem, recv_sem):
    span = pl.ds(SLOT_PARTS[part][0], len(SLOT_PARTS[part]))
    wait_blocks(
        src_ref.at[:, span], dst_ref.at[:, span], send_sem.at[part], recv_sem.at[part], NPLANE - 1
    )


def fill_table(order_ref, table_ref):
    angles = table_ref.shape[1]
    weight = math.sqrt(2.0 / angles)
    z = place()[2]
    row_id = lax.broadcasted_iota(jnp.int32, (128, 128), 0)
    lane = lax.broadcasted_iota(jnp.int32, (128, 128), 1)
    spot = row_id & (NZ - 1)
    step = (spot + 1) >> 1
    offset = NZ // 2 + jnp.where((spot & 1) == 1, -step, step)
    chosen = lane == row_id - spot + ((z + offset) & (NZ - 1))
    chosen = jnp.where(chosen, 1.0, 0.0).astype(jnp.bfloat16)
    for half in range(2):
        row = order_ref[half : half + 1, :].astype(jnp.float32)
        k = lax.dot_general(
            chosen,
            jnp.broadcast_to(row, (128, 128)).astype(jnp.bfloat16),
            (((1,), (1,)), ((), ())),
            preferred_element_type=jnp.float32,
        ).astype(jnp.int32)
        turn = (k * lane) & (angles - 1)
        quarter = (turn + angles // 8) >> 7
        angle = (turn - quarter * (angles // 4)).astype(jnp.float32) * (2.0 * math.pi / angles)
        sq = angle * angle
        cos = 1.0 + sq * (-1 / 2 + sq * (1 / 24 + sq * (-1 / 720 + sq * (1 / 40320))))
        sin = angle * (1.0 + sq * (-1 / 6 + sq * (1 / 120 + sq * (-1 / 5040 + sq * (1 / 362880)))))
        cos = cos * weight
        sin = sin * weight
        for b in range(angles // 128):
            quadrant = (quarter + b * k) & 3
            odd = (quadrant & 1) == 1
            upper = quadrant >= 2
            even_sign = jnp.where(upper, -1.0, 1.0)
            real = jnp.where(odd, -sin, cos) * even_sign
            imag = jnp.where(odd, -cos, -sin) * even_sign
            span = slice(128 * b, 128 * (b + 1))
            table_ref[128 * half : 128 * (half + 1), span] = real.astype(jnp.bfloat16)
            table_ref[256 + 128 * half : 256 + 128 * (half + 1), span] = imag.astype(jnp.bfloat16)


def fill_spectrum(table_ref, images_ref, wide_ref):
    slots = table_ref.shape[0] // 2
    for p in range(0, images_ref.shape[0], 2):
        pair = images_ref[p : p + 2].reshape(2 * images_ref.shape[1], images_ref.shape[2])
        for c in range(2):
            part = lax.dot_general(
                table_ref[slots * c : slots * (c + 1), :],
                pair,
                (((1,), (1,)), ((), ())),
                preferred_element_type=jnp.float32,
            )
            wide_ref[pl.ds(4 * c + p, slots, stride=8), :] = part[:, :128]
            wide_ref[pl.ds(4 * c + p + 1, slots, stride=8), :] = part[:, 128:]


def whole_kernel(
    images_in,
    radial_ref,
    first_in,
    count_in,
    order_in,
    start_ref,
    table_out,
    out_ref,
    images_ref,
    first_ref,
    count_ref,
    order_ref,
    table_ref,
    back_ref,
    wide_ref,
    spec_ref,
    rows_ref,
    radial_own,
    masked_ref,
    coef_ref,
    part_ref,
    given_ref,
    taken_ref,
    eigs_ref,
    prof_ref,
    start_own,
    send_1,
    recv_1,
    send_4,
    recv_4,
    send_3,
    recv_3,
    send_2,
    recv_2,
    own_1,
    own_4,
    load_1,
    load_2,
    store_1,
    load_3,
    load_4,
    load_5,
    load_6,
):
    d, o, z, y, x = place()
    first_slot = (y * NX + x) * NZ
    barrier = pltpu.get_barrier_semaphore()
    for _, _, pd in z_peers():
        pl.semaphore_signal(barrier, inc=1, device_id=(pd, o), device_id_type=MESH)
    for _, pd, po in plane_peers():
        pl.semaphore_signal(barrier, inc=1, device_id=(pd, po), device_id_type=MESH)
    order_load = pltpu.make_async_copy(order_in, order_ref, load_3)
    images_load = pltpu.make_async_copy(images_in, images_ref, load_4)
    first_load = pltpu.make_async_copy(first_in, first_ref, load_5)
    count_load = pltpu.make_async_copy(count_in, count_ref, load_6)
    order_load.start()
    images_load.start()
    first_load.start()
    count_load.start()
    radial_load = pltpu.make_async_copy(radial_ref.at[pl.ds(first_slot, NZ)], radial_own, load_1)
    start_load = pltpu.make_async_copy(start_ref.at[first_slot + z], start_own, load_2)
    radial_load.start()
    start_load.start()
    order_load.wait()
    fill_table(order_ref, table_ref)
    table_store = pltpu.make_async_copy(table_ref, table_out, store_1)
    table_store.start()
    images_load.wait()
    fill_spectrum(table_ref, images_ref, wide_ref)
    spec_ref[...] = wide_ref[...].reshape(spec_ref.shape).astype(jnp.bfloat16)
    radial_load.wait()
    start_load.wait()
    first_load.wait()
    count_load.wait()
    radial_rows, width = masked_ref.shape[1:]
    row_id = lax.broadcasted_iota(jnp.int32, (radial_rows, width), 0)
    col_id = lax.broadcasted_iota(jnp.int32, (radial_rows, width), 1)
    for i, k in enumerate(FAR_FIRST_8):
        j = (z + k) % NZ
        first_row = first_ref[first_slot + j] * (radial_rows // NRB)
        keep = (row_id >= first_row) & (col_id < count_ref[first_slot + j])
        masked = jnp.where(keep, radial_own[j].astype(jnp.float32), 0.0)
        masked_ref[i] = masked.astype(jnp.bfloat16)
    pl.semaphore_wait(barrier, NPLANE - 1 + NZ - 1)
    own = own_block(spec_ref, rows_ref, own_1)
    own.start()
    for part in range(len(SLOT_PARTS)):
        send_part(part, spec_ref, rows_ref, send_1, recv_1)
    own.wait()

    peers = list(z_peers())
    for part, spots in enumerate(SLOT_PARTS):
        wait_part(part, spec_ref, rows_ref, send_1, recv_1)
        for i in spots:
            rows = rows_ref[:, i].astype(jnp.float32).reshape(NPLANE * 8, radial_rows)
            coef = jnp.dot(
                rows.astype(jnp.bfloat16), masked_ref[i], preferred_element_type=jnp.float32
            ).astype(jnp.bfloat16)
            coef_ref[i] = coef
            cov = fold(
                lax.dot_general(
                    coef, coef, (((0,), (0,)), ((), ())), preferred_element_type=jnp.float32
                )
            )
            if i < len(peers):
                _, there, pd = peers[i]
                given_ref[i] = cov.astype(jnp.bfloat16)
                remote(given_ref.at[i], taken_ref.at[there], send_2, recv_2, (pd, o)).start()
            else:
                part_ref[...] = cov
    wait_blocks(given_ref, taken_ref, send_2, recv_2, NZ - 1)
    cov = part_ref[...]
    for i in range(NZ - 1):
        cov = cov + taken_ref[i].astype(jnp.float32)

    cov_high, cov_low = split(unfold(cov), 2)
    basis_t = start_own[...]
    for step in range(ITERS):
        basis_t = orthonormal(times_cov(basis_t, cov_high, cov_low))
    eig_t = basis_t.astype(jnp.bfloat16)
    eigs_ref[NZ - 1] = eig_t
    for i, there, pd in peers:
        remote(
            eigs_ref.at[NZ - 1], eigs_ref.at[there], send_3.at[i], recv_3.at[there], (pd, o)
        ).start()

    for part in reversed(range(len(SLOT_PARTS))):
        for i in reversed(SLOT_PARTS[part]):
            if i < len(peers):
                remote(
                    eigs_ref.at[i], eigs_ref.at[i], send_3.at[i], recv_3.at[i], (peers[i][2], o)
                ).wait_recv()
            eig_t = eigs_ref[i]
            u_t = lax.dot_general(
                eig_t, masked_ref[i], (((1,), (1,)), ((), ())), preferred_element_type=jnp.float32
            ).astype(jnp.bfloat16)
            scores = lax.dot_general(
                coef_ref[i], eig_t, (((1,), (1,)), ((), ())), preferred_element_type=jnp.float32
            ).astype(jnp.bfloat16)
            profile = jnp.dot(scores, u_t, preferred_element_type=jnp.float32)
            prof_ref[:, i] = profile.reshape(NPLANE, 8, radial_rows).astype(jnp.bfloat16)
        send_part(part, prof_ref, back_ref, send_4, recv_4)
    own = own_block(prof_ref, back_ref, own_4)
    own.start()
    for i, _, pd in peers:
        remote(
            eigs_ref.at[NZ - 1], eigs_ref.at[i], send_3.at[i], recv_3.at[i], (pd, o)
        ).wait_send()
    own.wait()

    by_slot = wide_ref.reshape(*back_ref.shape)
    for part in reversed(range(len(SLOT_PARTS))):
        wait_part(part, prof_ref, back_ref, send_4, recv_4)
        for i in SLOT_PARTS[part]:
            by_slot[:, i] = back_ref[:, i].astype(jnp.float32)
    slots = NPLANE * NZ
    for p in range(out_ref.shape[0]):
        for c in range(2):
            ordered = wide_ref[pl.ds(4 * c + p, slots, stride=8), :]
            out_ref[p, slots * c : slots * (c + 1), :] = ordered.astype(jnp.bfloat16)
    table_store.wait()


def on_device(polar_images, radial_basis, radial_start, radial_count, order_of_slot, start_block):
    particles, radial_rows, angles = polar_images.shape
    rank, width = start_block.shape[1:]
    slots = order_of_slot.shape[0]
    blocks = (NPLANE, NZ, 2 * particles, radial_rows)
    vmem = pl.BlockSpec(memory_space=pltpu.VMEM)
    anywhere = pl.BlockSpec(memory_space=pl.ANY)
    table, mine = pl.pallas_call(
        whole_kernel,
        out_shape=(
            jax.ShapeDtypeStruct((2 * slots, angles), jnp.bfloat16),
            jax.ShapeDtypeStruct((particles, 2 * slots, radial_rows), jnp.bfloat16),
        ),
        in_specs=[anywhere] * 6,
        out_specs=(anywhere, vmem),
        scratch_shapes=[
            pltpu.VMEM(polar_images.shape, jnp.bfloat16),
            pltpu.SMEM(radial_start.shape, jnp.int32),
            pltpu.SMEM(radial_count.shape, jnp.int32),
            pltpu.VMEM((2, slots // 2), jnp.int32),
            pltpu.VMEM((2 * slots, angles), jnp.bfloat16),
            pltpu.VMEM(blocks, jnp.bfloat16),
            pltpu.VMEM((slots * 2 * particles, radial_rows), jnp.float32),
            pltpu.VMEM(blocks, jnp.bfloat16),
            pltpu.VMEM(blocks, jnp.bfloat16),
            pltpu.VMEM((NZ, radial_rows, width), jnp.bfloat16),
            pltpu.VMEM((NZ, radial_rows, width), jnp.bfloat16),
            pltpu.VMEM((NZ, NPLANE * 2 * particles, width), jnp.bfloat16),
            pltpu.VMEM((80, width), jnp.float32),
            pltpu.VMEM((NZ, 80, width), jnp.bfloat16),
            pltpu.VMEM((NZ, 80, width), jnp.bfloat16),
            pltpu.VMEM((NZ, rank, width), jnp.bfloat16),
            pltpu.VMEM(blocks, jnp.bfloat16),
            pltpu.VMEM((rank, width), jnp.float32),
            *[pltpu.SemaphoreType.DMA((len(SLOT_PARTS),))] * 4,
            *[pltpu.SemaphoreType.DMA((NZ - 1,))] * 2,
            *[pltpu.SemaphoreType.DMA] * 11,
        ],
        compiler_params=pltpu.CompilerParams(collective_id=0, has_side_effects=True),
        name="whole",
    )(
        polar_images,
        radial_basis,
        radial_start,
        radial_count,
        order_of_slot.reshape(2, slots // 2),
        start_block,
    )
    denoised = jnp.einsum("per,et->prt", mine, table, preferred_element_type=jnp.float32)
    return denoised.astype(jnp.bfloat16)


def solution(mesh):
    placed = (
        P(("dom", "ord"), None, None),
        P("ord", None, None),
        P("ord"),
        P("ord"),
        P(),
        P("ord", None, None),
    )
    return jax.shard_map(
        on_device,
        mesh=mesh,
        in_specs=placed,
        out_specs=P(("dom", "ord"), None, None),
        check_vma=False,
    )
```

```python
import math

import jax
import jax.numpy as jnp
from jax import lax
from jax.experimental import pallas as pl
from jax.experimental.pallas import tpu as pltpu
from jax.sharding import PartitionSpec as P

NRB = 8
ITERS = 4
NZ, NY, NX = 8, 4, 4
NDOM = NZ * NY * NX
NPLANE = 2 * NY * NX
MESH = pl.DeviceIdType.MESH


FAR_FIRST_8 = (4, 3, 5, 2, 6, 1, 7, 0)
FAR_FIRST_4 = (2, 1, 3, 0)
SLOT_PARTS = ((0, 1), (2, 3), (4, 5), (6, 7))


def dot32(a, b, dims):
    return lax.dot_general(
        a, b, (dims, ((), ())), precision=lax.Precision.HIGHEST, preferred_element_type=jnp.float32
    )


def split(value, pieces):
    out = []
    for _ in range(pieces):
        piece = value.astype(jnp.bfloat16)
        value = value - piece.astype(jnp.float32)
        out.append(piece)
    return out


def times_cov(basis_t, cov_high, cov_low):
    rank = basis_t.shape[0]
    high, low = split(basis_t, 2)
    both = jnp.dot(
        jnp.concatenate([high, low], axis=0), cov_high, preferred_element_type=jnp.float32
    )
    rest = jnp.dot(high, cov_low, preferred_element_type=jnp.float32)
    return both[:rank] + (both[rank:] + rest)


def fold(cov):
    lane = lax.broadcasted_iota(jnp.int32, (32, 128), 1)
    second = jnp.where(lane < 32, pltpu.roll(cov[96:], 32, 1), cov[32:64])
    third = jnp.where(lane[:16] < 64, pltpu.roll(cov[80:96], 64, 1), cov[64:80])
    return jnp.concatenate([cov[:32], second, third], axis=0)


def unfold(folded):
    second, third = folded[32:64], folded[64:]
    upper = jnp.concatenate(
        [folded[:32], second, third, pltpu.roll(third, 64, 1), pltpu.roll(second, 96, 1)], axis=0
    )
    row_block = lax.broadcasted_iota(jnp.int32, (128, 128), 0) // 32
    lane_block = lax.broadcasted_iota(jnp.int32, (128, 128), 1) // 32
    return jnp.where(row_block > lane_block, upper.T, upper)


def orthonormal(image_t):
    rank, width = image_t.shape
    gram = dot32(image_t, image_t, ((1,), (1,)))
    lane_block = lax.broadcasted_iota(jnp.int32, (rank, rank * width), 1) // width
    spread = lane_block == lax.broadcasted_iota(jnp.int32, (rank, rank * width), 0)
    pieces = jnp.concatenate(split(gram, 3), axis=0)
    wide = jnp.dot(
        pieces, jnp.where(spread, 1.0, 0.0).astype(jnp.bfloat16), preferred_element_type=jnp.float32
    )
    wide = wide[:rank] + wide[rank : 2 * rank] + wide[2 * rank :]
    cols = [wide[:, j * width : (j + 1) * width] for j in range(rank)]
    row_id = lax.broadcasted_iota(jnp.int32, (rank, width), 0)
    pivots = jnp.ones((rank, width), jnp.float32)
    out = image_t
    for j in range(rank):
        pivot = jnp.broadcast_to(cols[j][j : j + 1, :], (rank, width))
        pivots = jnp.where(row_id == j, pivot, pivots)
        factor = jnp.where(row_id > j, cols[j] / pivot, 0.0)
        for k in range(j + 1, rank):
            cols[k] = cols[k] - factor * cols[k][j : j + 1, :]
        out = out - factor * out[j : j + 1, :]
    return out / jnp.sqrt(pivots)


def place():
    d = lax.axis_index("dom")
    return d, lax.axis_index("ord"), d // (NY * NX), (d // NX) % NY, d % NX


def z_peers():
    d, o, z, y, x = place()
    for i, k in enumerate(FAR_FIRST_8[:-1]):
        pd = (z + k) % NZ * (NY * NX) + y * NX + x
        yield i, FAR_FIRST_8.index((NZ - k) % NZ), pd


def plane_peers():
    d, o, z, y, x = place()
    at_y = [(y + k) % NY * NX for k in range(NY)]
    at_x = [(x + k) % NX for k in range(NX)]
    for dy in FAR_FIRST_4:
        for dx in FAR_FIRST_4:
            m = at_y[dy] + at_x[dx]
            for po in (1 - o, o) if (dy, dx) != (0, 0) else (1 - o,):
                yield po * (NY * NX) + m, z * (NY * NX) + m, po


def remote(src_ref, dst_ref, send_sem, recv_sem, device):
    return pltpu.make_async_remote_copy(
        src_ref=src_ref,
        dst_ref=dst_ref,
        send_sem=send_sem,
        recv_sem=recv_sem,
        device_id=device,
        device_id_type=MESH,
    )


def wait_blocks(src_ref, dst_ref, send_sem, recv_sem, blocks):
    d, o = place()[:2]
    most = pl.ds(0, blocks)
    everything = remote(src_ref.at[most], dst_ref.at[most], send_sem, recv_sem, (d, 1 - o))
    everything.wait_send()
    everything.wait_recv()


def own_block(src_ref, dst_ref, own_sem):
    d, o, z, y, x = place()
    mine = o * (NY * NX) + y * NX + x
    return pltpu.make_async_copy(src_ref.at[mine], dst_ref.at[mine], own_sem)


def send_part(part, src_ref, dst_ref, send_sem, recv_sem):
    d, o, z, y, x = place()
    mine = o * (NY * NX) + y * NX + x
    span = pl.ds(SLOT_PARTS[part][0], len(SLOT_PARTS[part]))
    for index, pd, po in plane_peers():
        remote(
            src_ref.at[index, span],
            dst_ref.at[mine, span],
            send_sem.at[part],
            recv_sem.at[part],
            (pd, po),
        ).start()


def wait_part(part, src_ref, dst_ref, send_sem, recv_sem):
    span = pl.ds(SLOT_PARTS[part][0], len(SLOT_PARTS[part]))
    wait_blocks(
        src_ref.at[:, span], dst_ref.at[:, span], send_sem.at[part], recv_sem.at[part], NPLANE - 1
    )


def fill_table(order_ref, table_ref):
    angles = table_ref.shape[1]
    weight = math.sqrt(2.0 / angles)
    z = place()[2]
    row_id = lax.broadcasted_iota(jnp.int32, (128, 128), 0)
    lane = lax.broadcasted_iota(jnp.int32, (128, 128), 1)
    spot = row_id & (NZ - 1)
    step = (spot + 1) >> 1
    offset = NZ // 2 + jnp.where((spot & 1) == 1, -step, step)
    chosen = lane == row_id - spot + ((z + offset) & (NZ - 1))
    chosen = jnp.where(chosen, 1.0, 0.0).astype(jnp.bfloat16)
    for half in range(2):
        row = order_ref[half : half + 1, :].astype(jnp.float32)
        k = lax.dot_general(
            chosen,
            jnp.broadcast_to(row, (128, 128)).astype(jnp.bfloat16),
            (((1,), (1,)), ((), ())),
            preferred_element_type=jnp.float32,
        ).astype(jnp.int32)
        turn = (k * lane) & (angles - 1)
        quarter = (turn + angles // 8) >> 7
        angle = (turn - quarter * (angles // 4)).astype(jnp.float32) * (2.0 * math.pi / angles)
        sq = angle * angle
        cos = 1.0 + sq * (-1 / 2 + sq * (1 / 24 + sq * (-1 / 720 + sq * (1 / 40320))))
        sin = angle * (1.0 + sq * (-1 / 6 + sq * (1 / 120 + sq * (-1 / 5040 + sq * (1 / 362880)))))
        cos = cos * weight
        sin = sin * weight
        for b in range(angles // 128):
            quadrant = (quarter + b * k) & 3
            odd = (quadrant & 1) == 1
            upper = quadrant >= 2
            even_sign = jnp.where(upper, -1.0, 1.0)
            real = jnp.where(odd, -sin, cos) * even_sign
            imag = jnp.where(odd, -cos, -sin) * even_sign
            span = slice(128 * b, 128 * (b + 1))
            table_ref[128 * half : 128 * (half + 1), span] = real.astype(jnp.bfloat16)
            table_ref[256 + 128 * half : 256 + 128 * (half + 1), span] = imag.astype(jnp.bfloat16)


def fill_spectrum(table_ref, images_ref, wide_ref):
    slots = table_ref.shape[0] // 2
    for p in range(0, images_ref.shape[0], 2):
        pair = images_ref[p : p + 2].reshape(2 * images_ref.shape[1], images_ref.shape[2])
        for c in range(2):
            part = lax.dot_general(
                table_ref[slots * c : slots * (c + 1), :],
                pair,
                (((1,), (1,)), ((), ())),
                preferred_element_type=jnp.float32,
            )
            wide_ref[pl.ds(4 * c + p, slots, stride=8), :] = part[:, :128]
            wide_ref[pl.ds(4 * c + p + 1, slots, stride=8), :] = part[:, 128:]


def whole_kernel(
    images_in,
    radial_ref,
    first_in,
    count_in,
    order_in,
    start_ref,
    table_out,
    profile_out,
    out_ref,
    images_ref,
    first_ref,
    count_ref,
    order_ref,
    table_ref,
    back_ref,
    wide_ref,
    spec_ref,
    rows_ref,
    radial_own,
    masked_ref,
    coef_ref,
    part_ref,
    given_ref,
    taken_ref,
    eigs_ref,
    prof_ref,
    start_own,
    send_1,
    recv_1,
    send_4,
    recv_4,
    send_3,
    recv_3,
    send_2,
    recv_2,
    own_1,
    own_4,
    load_1,
    load_2,
    store_1,
    load_3,
    load_4,
    load_5,
    load_6,
    store_2,
):
    d, o, z, y, x = place()
    first_slot = (y * NX + x) * NZ
    barrier = pltpu.get_barrier_semaphore()
    for _, _, pd in z_peers():
        pl.semaphore_signal(barrier, inc=1, device_id=(pd, o), device_id_type=MESH)
    for _, pd, po in plane_peers():
        pl.semaphore_signal(barrier, inc=1, device_id=(pd, po), device_id_type=MESH)
    order_load = pltpu.make_async_copy(order_in, order_ref, load_3)
    images_load = pltpu.make_async_copy(images_in, images_ref, load_4)
    first_load = pltpu.make_async_copy(first_in, first_ref, load_5)
    count_load = pltpu.make_async_copy(count_in, count_ref, load_6)
    order_load.start()
    images_load.start()
    first_load.start()
    count_load.start()
    radial_load = pltpu.make_async_copy(radial_ref.at[pl.ds(first_slot, NZ)], radial_own, load_1)
    start_load = pltpu.make_async_copy(start_ref.at[first_slot + z], start_own, load_2)
    radial_load.start()
    start_load.start()
    order_load.wait()
    fill_table(order_ref, table_ref)
    table_store = pltpu.make_async_copy(table_ref, table_out, store_1)
    table_store.start()
    images_load.wait()
    fill_spectrum(table_ref, images_ref, wide_ref)
    spec_ref[...] = wide_ref[...].reshape(spec_ref.shape).astype(jnp.bfloat16)
    radial_load.wait()
    start_load.wait()
    first_load.wait()
    count_load.wait()
    radial_rows, width = masked_ref.shape[1:]
    row_id = lax.broadcasted_iota(jnp.int32, (radial_rows, width), 0)
    col_id = lax.broadcasted_iota(jnp.int32, (radial_rows, width), 1)
    for i, k in enumerate(FAR_FIRST_8):
        j = (z + k) % NZ
        first_row = first_ref[first_slot + j] * (radial_rows // NRB)
        keep = (row_id >= first_row) & (col_id < count_ref[first_slot + j])
        masked = jnp.where(keep, radial_own[j].astype(jnp.float32), 0.0)
        masked_ref[i] = masked.astype(jnp.bfloat16)
    pl.semaphore_wait(barrier, NPLANE - 1 + NZ - 1)
    own = own_block(spec_ref, rows_ref, own_1)
    own.start()
    for part in range(len(SLOT_PARTS)):
        send_part(part, spec_ref, rows_ref, send_1, recv_1)
    own.wait()

    peers = list(z_peers())
    for part, spots in enumerate(SLOT_PARTS):
        wait_part(part, spec_ref, rows_ref, send_1, recv_1)
        for i in spots:
            rows = rows_ref[:, i].astype(jnp.float32).reshape(NPLANE * 8, radial_rows)
            coef = jnp.dot(
                rows.astype(jnp.bfloat16), masked_ref[i], preferred_element_type=jnp.float32
            ).astype(jnp.bfloat16)
            coef_ref[i] = coef
            cov = fold(
                lax.dot_general(
                    coef, coef, (((0,), (0,)), ((), ())), preferred_element_type=jnp.float32
                )
            )
            if i < len(peers):
                _, there, pd = peers[i]
                given_ref[i] = cov.astype(jnp.bfloat16)
                remote(given_ref.at[i], taken_ref.at[there], send_2, recv_2, (pd, o)).start()
            else:
                part_ref[...] = cov
    wait_blocks(given_ref, taken_ref, send_2, recv_2, NZ - 1)
    cov = part_ref[...]
    for i in range(NZ - 1):
        cov = cov + taken_ref[i].astype(jnp.float32)

    cov_high, cov_low = split(unfold(cov), 2)
    basis_t = start_own[...]
    for step in range(ITERS):
        basis_t = orthonormal(times_cov(basis_t, cov_high, cov_low))
    eig_t = basis_t.astype(jnp.bfloat16)
    eigs_ref[NZ - 1] = eig_t
    for i, there, pd in peers:
        remote(
            eigs_ref.at[NZ - 1], eigs_ref.at[there], send_3.at[i], recv_3.at[there], (pd, o)
        ).start()

    for part in reversed(range(len(SLOT_PARTS))):
        for i in reversed(SLOT_PARTS[part]):
            if i < len(peers):
                remote(
                    eigs_ref.at[i], eigs_ref.at[i], send_3.at[i], recv_3.at[i], (peers[i][2], o)
                ).wait_recv()
            eig_t = eigs_ref[i]
            u_t = lax.dot_general(
                eig_t, masked_ref[i], (((1,), (1,)), ((), ())), preferred_element_type=jnp.float32
            ).astype(jnp.bfloat16)
            scores = lax.dot_general(
                coef_ref[i], eig_t, (((1,), (1,)), ((), ())), preferred_element_type=jnp.float32
            ).astype(jnp.bfloat16)
            profile = jnp.dot(scores, u_t, preferred_element_type=jnp.float32)
            prof_ref[:, i] = profile.reshape(NPLANE, 8, radial_rows).astype(jnp.bfloat16)
        send_part(part, prof_ref, back_ref, send_4, recv_4)
    own = own_block(prof_ref, back_ref, own_4)
    own.start()
    for i, _, pd in peers:
        remote(
            eigs_ref.at[NZ - 1], eigs_ref.at[i], send_3.at[i], recv_3.at[i], (pd, o)
        ).wait_send()
    own.wait()

    by_slot = wide_ref.reshape(*back_ref.shape)
    for part in reversed(range(len(SLOT_PARTS))):
        wait_part(part, prof_ref, back_ref, send_4, recv_4)
        for i in SLOT_PARTS[part]:
            by_slot[:, i] = back_ref[:, i].astype(jnp.float32)
    slots = NPLANE * NZ
    stores = []
    for p in range(out_ref.shape[0]):
        for c in range(2):
            ordered = wide_ref[pl.ds(4 * c + p, slots, stride=8), :]
            out_ref[p, slots * c : slots * (c + 1), :] = ordered.astype(jnp.bfloat16)
        stores.append(pltpu.make_async_copy(out_ref.at[p], profile_out.at[p], store_2.at[p]))
        stores[-1].start()
    for store in stores:
        store.wait()
    table_store.wait()


def on_device(polar_images, radial_basis, radial_start, radial_count, order_of_slot, start_block):
    particles, radial_rows, angles = polar_images.shape
    rank, width = start_block.shape[1:]
    slots = order_of_slot.shape[0]
    blocks = (NPLANE, NZ, 2 * particles, radial_rows)
    anywhere = pl.BlockSpec(memory_space=pl.ANY)
    table, mine = pl.pallas_call(
        whole_kernel,
        out_shape=(
            jax.ShapeDtypeStruct((2 * slots, angles), jnp.bfloat16),
            jax.ShapeDtypeStruct((particles, 2 * slots, radial_rows), jnp.bfloat16),
        ),
        in_specs=[anywhere] * 6,
        out_specs=(anywhere, anywhere),
        scratch_shapes=[
            pltpu.VMEM((particles, 2 * slots, radial_rows), jnp.bfloat16),
            pltpu.VMEM(polar_images.shape, jnp.bfloat16),
            pltpu.SMEM(radial_start.shape, jnp.int32),
            pltpu.SMEM(radial_count.shape, jnp.int32),
            pltpu.VMEM((2, slots // 2), jnp.int32),
            pltpu.VMEM((2 * slots, angles), jnp.bfloat16),
            pltpu.VMEM(blocks, jnp.bfloat16),
            pltpu.VMEM((slots * 2 * particles, radial_rows), jnp.float32),
            pltpu.VMEM(blocks, jnp.bfloat16),
            pltpu.VMEM(blocks, jnp.bfloat16),
            pltpu.VMEM((NZ, radial_rows, width), jnp.bfloat16),
            pltpu.VMEM((NZ, radial_rows, width), jnp.bfloat16),
            pltpu.VMEM((NZ, NPLANE * 2 * particles, width), jnp.bfloat16),
            pltpu.VMEM((80, width), jnp.float32),
            pltpu.VMEM((NZ, 80, width), jnp.bfloat16),
            pltpu.VMEM((NZ, 80, width), jnp.bfloat16),
            pltpu.VMEM((NZ, rank, width), jnp.bfloat16),
            pltpu.VMEM(blocks, jnp.bfloat16),
            pltpu.VMEM((rank, width), jnp.float32),
            *[pltpu.SemaphoreType.DMA((len(SLOT_PARTS),))] * 4,
            *[pltpu.SemaphoreType.DMA((NZ - 1,))] * 2,
            *[pltpu.SemaphoreType.DMA] * 11,
            pltpu.SemaphoreType.DMA((particles,)),
        ],
        compiler_params=pltpu.CompilerParams(collective_id=0, has_side_effects=True),
        name="whole",
    )(
        polar_images,
        radial_basis,
        radial_start,
        radial_count,
        order_of_slot.reshape(2, slots // 2),
        start_block,
    )
    denoised = jnp.einsum("per,et->prt", mine, table, preferred_element_type=jnp.float32)
    return denoised.astype(jnp.bfloat16)


def solution(mesh):
    placed = (
        P(("dom", "ord"), None, None),
        P("ord", None, None),
        P("ord"),
        P("ord"),
        P(),
        P("ord", None, None),
    )
    return jax.shard_map(
        on_device,
        mesh=mesh,
        in_specs=placed,
        out_specs=P(("dom", "ord"), None, None),
        check_vma=False,
    )
```
